32 devices in a mesh: seq: 16 (over z, y, x), head: 2 (over core).
Axes of the slice: x: 2, y: 2, z: 4, core: 2. Of those that a mesh axis runs over, the one named last changes fastest.
Arguments:
- tokens: bfloat16 [10240, 768], P('seq', 'head'), may hold values from -6 to 6
- image_starts: int32 [54], replicated, may hold values from 0 to 10240, as said below
- ln_gain: float32 [768], replicated, may hold values from 0.1 to 1.9
- w_qkv: bfloat16 [768, 3, 768], P(None, None, 'head'), may hold values from -0.21875 to 0.21875
- q_gain: float32 [64], replicated, may hold values from 0.8 to 2
- k_gain: float32 [64], replicated, may hold values from 0.8 to 2
- w_up: bfloat16 [768, 3072], P(None, 'head'), may hold values from -0.21875 to 0.21875
- up_bias: float32 [3072], P('head'), may hold values from -3 to 3
- w_attn_out: bfloat16 [768, 768], P('head'), may hold values from -1.25 to 1.25
- w_down: bfloat16 [3072, 768], P('head'), may hold values from -0.109375 to 0.109375
- out_bias: float32 [768], P('head'), may hold values from -3 to 3
- cotangent: bfloat16 [10240, 768], P('seq', 'head'), may hold values from -8 to 8
Outputs:
- block_out: bfloat16 [10240, 768], P('seq', 'head')
- tokens_grad: bfloat16 [10240, 768], P('seq', 'head')
- ln_gain_grad: float32 [768], P('head')
- w_qkv_grad: float32 [768, 3, 768], P(None, None, 'head')
- q_gain_grad: float32 [64], P('head')
- k_gain_grad: float32 [64], P('head')
- w_up_grad: float32 [768, 3072], P(None, 'head')
- up_bias_grad: float32 [3072], P('head')
- w_attn_out_grad: float32 [768, 768], P('head')
- w_down_grad: float32 [3072, 768], P('head')
- out_bias_grad: float32 [768], P('head')
The draws below stay inside these ranges and needn't reach their ends.
Inputs may be any that keep to these rules, and one draw needn't show every extreme that they name: image_starts[0] is 0 and the entries rise strictly until they reach 10240; all later entries equal 10240 and are unused. Image i holds the tokens from its start up to the next entry minus one; every image holds 196 or 3136 tokens except the last, which may be cut short, and at least one holds exactly 3136.
All inputs are finite; a program needn't handle non-finite values.
Results may differ from the reference program's by a relative error of at most 0.012.
Values may be sent and summed in bfloat16 or wider, within the bound.
No kernel may reach another device: no remote copies, remote signals or barrier semaphores. Data moves between devices by JAX's collectives and lax.ppermute only.
A program may use at most 192 MiB of HBM per device.

```python
import jax
import jax.numpy as jnp
from jax import lax

D = 768
HEADS = 12
HS = 64
FF = 3072
TOK_DEV = 640
SHORT_LEN = 196
LONG_LEN = 3136
TOKENS = 10240
REACH = 5
N_SEQ = 16


def draw_image_starts(key, part):
    slot_count = TOKENS // SHORT_LEN + 2
    base_key = jax.random.fold_in(key, 7)
    key_rolls = jax.random.fold_in(base_key, 11)
    key_extra = jax.random.fold_in(base_key, 13)
    key_forced = jax.random.fold_in(base_key, 17)
    long_rolls = jax.random.randint(key_rolls, (slot_count,), 0, 12)
    extra_rolls = jax.random.randint(key_extra, (slot_count,), 0, 12)
    forced = jax.random.randint(key_forced, (), 0, 3)
    slot_index = jnp.arange(slot_count, dtype=jnp.int32)
    is_long = (long_rolls == 0) | (extra_rolls == 1) | (slot_index == forced)
    is_long = jnp.where(slot_index < forced, False, is_long)
    lengths = jnp.where(is_long, LONG_LEN, SHORT_LEN).astype(jnp.int32)
    image_ends = jnp.cumsum(lengths).astype(jnp.int32)
    starts = jnp.concatenate([jnp.zeros((1,), jnp.int32), image_ends[:-1]])
    return jnp.minimum(starts, TOKENS).astype(jnp.int32)


def draw_cotangent(key, part):
    row_index = jnp.arange(TOKENS, dtype=jnp.float32)[:, None]
    position_ramp = row_index / max(TOKENS - 1, 1)
    raw_noise = jax.random.truncated_normal(jax.random.fold_in(key, 3), -4.0, 4.0, (TOKENS, D), jnp.float32)
    factor = 0.6 * 3.0 ** position_ramp
    return (raw_noise * factor).astype(jnp.bfloat16)


def level_of(stream_key, shape, cuts, smallest, top_value):
    level = 1.0
    for position, blocks in cuts:
        draws = jax.random.uniform(jax.random.fold_in(jax.random.fold_in(stream_key, 6), position), (blocks,), jnp.float32, smallest / len(cuts), top_value / len(cuts))
        level = level * jnp.repeat(jnp.exp(draws), shape[position] // blocks).reshape((-1,) + (1,) * (len(shape) - 1 - position))
    return level


def gaussian(key, extent, deviation, most, shards=(), kind=jnp.bfloat16):
    gain = level_of(key, extent, shards, -0.22, 0.18) if shards else 1.0
    result = jax.random.normal(key, extent, jnp.float32) * deviation * gain
    return jnp.minimum(jnp.maximum(result, -most), most).astype(kind)


def setup_inputs(seed: int = 0) -> dict:
    seeds = jax.random.split(jax.random.key(seed), 13)
    return {
        "tokens": gaussian(seeds[0], (TOKENS, D), 1.0, 6.0, ((0, 16), (1, 2))),
        "image_starts": draw_image_starts(jax.random.fold_in(seeds[12], 71), 0),
        "ln_gain": jnp.clip(1.0 + 0.18 * jax.random.normal(seeds[2], (D,), jnp.float32), 0.1, 1.9),
        "w_qkv": gaussian(seeds[3], (D, 3, D), D ** -0.5, 0.21875, ((2, 2),)),
        "q_gain": jnp.clip(jax.random.uniform(seeds[4], (HS,), jnp.float32, 0.8, 2.0), 0.8, 2.0),
        "k_gain": jnp.clip(jax.random.uniform(seeds[5], (HS,), jnp.float32, 0.8, 2.0), 0.8, 2.0),
        "w_up": gaussian(seeds[6], (D, FF), D ** -0.5, 0.21875, ((1, 2),)),
        "up_bias": gaussian(seeds[7], (FF,), 0.5, 3.0, ((0, 2),), jnp.float32),
        "w_attn_out": gaussian(seeds[8], (D, D), (D // 32) ** -0.5, 1.25, ((0, 2),)),
        "w_down": gaussian(seeds[9], (FF, D), FF ** -0.5, 0.109375, ((0, 2),)),
        "out_bias": gaussian(seeds[10], (D,), 0.5, 3.0, ((0, 2),), jnp.float32),
        "cotangent": draw_cotangent(jax.random.fold_in(seeds[12], 71), 0),
    }


EPSILON = 1e-06
MASKED = -1e+30
PRECISE = lax.Precision.HIGHEST

@jax.custom_vjp
def low(v):
    return lax.optimization_barrier(v.astype(jnp.bfloat16)).astype(jnp.float32)

@jax.custom_vjp
def low_back(v):
    return v

def low_keep(v):
    return (low(v), None)

def low_pass(kept, grad):
    return (grad,)

def back_keep(v):
    return (v, None)

def back_low(kept, grad):
    return (low(grad),)
low.defvjp(low_keep, low_pass)
low_back.defvjp(back_keep, back_low)

def layer_norm(values, gain_row):
    row_mean = lax.optimization_barrier(jnp.mean(values, axis=-1, keepdims=True))
    centred = values - row_mean
    spread = lax.optimization_barrier(jnp.mean(centred * centred, axis=-1, keepdims=True))
    return centred * lax.rsqrt(spread + EPSILON) * gain_row

def image_ids(image_starts, positions):
    return lax.optimization_barrier(jnp.sum((image_starts[None, :] <= positions[:, None]).astype(jnp.int32), axis=1))

def attend(queries, key_heads, values, query_images, key_images):
    scores = jnp.einsum('qhc,khc->hqk', queries, key_heads, precision=PRECISE)
    scores = low_back(scores)
    same_image = query_images[:, None] == key_images[None, :]
    masked = jnp.where(same_image[None], scores, MASKED)
    log_total = jax.nn.logsumexp(masked, axis=-1, keepdims=True)
    weights = low(jnp.exp(masked - log_total))
    return jnp.einsum('hqk,khc->qhc', weights, values, precision=PRECISE)

def forward(tokens, ln_gain, w_qkv, q_gain, k_gain, w_up, up_bias, w_attn_out, w_down, out_bias, token_images):
    normed = low(layer_norm(tokens, ln_gain))
    projected = jnp.einsum('td,dkc->tkc', normed, w_qkv, precision=PRECISE)
    shaped = (TOKENS, HEADS, HS)
    queries = low(layer_norm(low_back(projected[:, 0]).reshape(shaped), q_gain) * HS ** (-0.5))
    key_heads = low(layer_norm(low_back(projected[:, 1]).reshape(shaped), k_gain))
    values = low(low_back(projected[:, 2])).reshape(shaped)
    up_input = low_back(jnp.dot(normed, w_up, precision=PRECISE) + up_bias)
    hidden = low(jax.nn.gelu(up_input, approximate=False))
    margin = REACH * TOK_DEV
    pad_rows = ((margin, margin), (0, 0), (0, 0))
    keys_pad = jnp.pad(key_heads, pad_rows)
    values_pad = jnp.pad(values, pad_rows)
    images_pad = jnp.pad(token_images, (margin, margin), constant_values=-1)
    window = (2 * REACH + 1) * TOK_DEV

    def one_block(block_index):
        row_start = (block_index * TOK_DEV).astype(jnp.int32)
        q_rows = lax.dynamic_slice_in_dim(queries, row_start, TOK_DEV, 0)
        q_images = lax.dynamic_slice_in_dim(token_images, row_start, TOK_DEV, 0)
        k_rows = lax.dynamic_slice_in_dim(keys_pad, row_start, window, 0)
        v_rows = lax.dynamic_slice_in_dim(values_pad, row_start, window, 0)
        k_images = lax.dynamic_slice_in_dim(images_pad, row_start, window, 0)
        return attend(q_rows, k_rows, v_rows, q_images, k_images)
    mixture = lax.map(jax.checkpoint(one_block), jnp.arange(N_SEQ, dtype=jnp.int32))
    attended = low_back(low(mixture.reshape(TOKENS, D)))
    return tokens + jnp.dot(attended, w_attn_out, precision=PRECISE) + jnp.dot(hidden, w_down, precision=PRECISE) + out_bias

def reference(tokens, image_starts, ln_gain, w_qkv, q_gain, k_gain, w_up, up_bias, w_attn_out, w_down, out_bias, cotangent):
    positions = jnp.arange(TOKENS, dtype=jnp.int32)
    token_images = image_ids(image_starts, positions)

    def apply_layer(*params):
        return forward(*params, token_images)
    primals = (tokens.astype(jnp.float32), ln_gain, w_qkv.astype(jnp.float32), q_gain, k_gain, w_up.astype(jnp.float32), up_bias, w_attn_out.astype(jnp.float32), w_down.astype(jnp.float32), out_bias)
    output, pullback = jax.vjp(apply_layer, *primals)
    gradients = pullback(cotangent.astype(jnp.float32))
    return (output.astype(jnp.bfloat16), gradients[0].astype(jnp.bfloat16), gradients[1], gradients[2], gradients[3], gradients[4], gradients[5], gradients[6], gradients[7], gradients[8], gradients[9])
```

```python
import functools

import jax
import jax.numpy as jnp
from jax import lax
from jax.experimental import pallas as pl
from jax.experimental.pallas import tpu as pltpu
from jax.sharding import PartitionSpec as P

HS = 64
LONG_LEN = 3136
EPSILON = 1e-06
F32 = jnp.float32
BF16 = jnp.bfloat16
TILE = 256
VMEM_LIMIT = 60 * 1024 * 1024


def layer_norm(values, gain_row):
    row_mean = jnp.mean(values, axis=-1, keepdims=True)
    centred = values - row_mean
    spread = jnp.mean(centred * centred, axis=-1, keepdims=True)
    return centred * lax.rsqrt(spread + EPSILON) * gain_row


def exact_gelu(values):
    return jax.nn.gelu(values, approximate=False)


def dot_nn(a, b):
    return lax.dot_general(a, b, (((1,), (0,)), ((), ())), preferred_element_type=F32)


def dot_nt(a, b):
    return lax.dot_general(a, b, (((1,), (1,)), ((), ())), preferred_element_type=F32)


def dot_tn(a, b):
    return lax.dot_general(a, b, (((0,), (0,)), ((), ())), preferred_element_type=F32)


def half_means(block):
    left = lax.broadcasted_iota(jnp.int32, (128, 128), 0) // HS
    right = lax.broadcasted_iota(jnp.int32, (128, 128), 1) // HS
    averager = jnp.where(left == right, 1.0 / HS, 0.0).astype(F32)
    return lax.dot_general(
        block,
        averager,
        (((1,), (0,)), ((), ())),
        precision=lax.Precision.HIGHEST,
        preferred_element_type=F32,
    )


def normalized_halves(block):
    centred = block - half_means(block)
    inverse = lax.rsqrt(half_means(centred * centred) + EPSILON)
    return centred * inverse, inverse


def work_table(image_starts, place, n_seq, tok_rows, reach):
    window = reach + 1
    total = n_seq * tok_rows
    candidates = jnp.arange(2 * reach, dtype=jnp.int32) + place - reach
    positions = jnp.concatenate(
        [(candidates + 1) * tok_rows - 1, jnp.stack([place * tok_rows, (place + 1) * tok_rows - 1])]
    )
    below = image_starts[None, :] <= positions[:, None]
    starts = jnp.max(jnp.where(below, image_starts[None, :], -1), axis=1)
    ends = jnp.min(jnp.where(below, total, image_starts[None, :]), axis=1)
    first = starts // tok_rows
    last = (ends - 1) // tok_rows
    base = jnp.minimum(first, n_seq - window)
    spans = last > first
    mine = (
        (candidates >= 0)
        & (candidates < n_seq)
        & (first[:-2] == candidates)
        & spans[:-2]
        & (base[:-2] <= place)
        & (base[:-2] >= place - reach)
    )
    lengths = jnp.where(mine, ends[:-2] - starts[:-2], 0)
    rows = jnp.where(mine, starts[:-2] - (place - reach) * tok_rows, 0)
    low_end = jnp.where(spans[-2], jnp.clip(ends[-2] - place * tok_rows, 0, tok_rows), 0)
    low_end = jnp.where(first[-2] < place, low_end, 0)
    high_start = jnp.clip(starts[-1] - place * tok_rows, 0, tok_rows)
    high_start = jnp.where(last[-1] > place, high_start, tok_rows)
    head_part = jnp.stack([low_end, high_start, place - base[-2], place - base[-1]])
    return jnp.concatenate([head_part, rows, lengths]).astype(jnp.int32)


def pack_kernel(heads, reach, table, proj, datt, gains, *outs):
    slots, local = outs[:-1], outs[-1]
    rows = proj.shape[1]
    low = lax.broadcasted_iota(jnp.int32, (rows, 128), 1) < HS
    q_gain = gains[0:1, :] * (HS**-0.5)
    k_gain = gains[1:2, :]
    for pair in range(heads // 2):
        lanes = slice(pair * 128, (pair + 1) * 128)
        q = normalized_halves(proj[0, :, lanes])[0] * q_gain
        k = normalized_halves(proj[1, :, lanes])[0] * k_gain
        v = proj[2, :, lanes]
        d = datt[:, lanes].astype(F32)
        q, k, v = (t.astype(BF16).astype(F32) for t in (q, k, v))
        local[2 * pair, :, 0:128] = jnp.where(low, q, pltpu.roll(k, HS, 1)).astype(BF16)
        local[2 * pair, :, 128:256] = jnp.where(low, v, pltpu.roll(d, HS, 1)).astype(BF16)
        local[2 * pair + 1, :, 0:128] = jnp.where(low, pltpu.roll(q, HS, 1), k).astype(BF16)
        local[2 * pair + 1, :, 128:256] = jnp.where(low, pltpu.roll(v, HS, 1), d).astype(BF16)
    low_end = table[0]
    from_low = lax.broadcasted_iota(jnp.int32, (rows, 256), 0) < low_end
    for index, slot in enumerate(slots):
        distance = index - reach
        low_head = jnp.clip(table[2] + distance, 0, heads - 1)
        high_head = jnp.clip(table[3] + distance, 0, heads - 1)
        picked = jnp.where(from_low, local[low_head].astype(F32), local[high_head].astype(F32))
        slot[...] = picked.astype(BF16)


def softmax_tail(mixed, d_out):
    lane = lax.broadcasted_iota(jnp.int32, mixed.shape, 1)
    total = mixed[:, HS : HS + 1]
    inverse = 1.0 / jnp.where(total > 0, total, 1.0)
    mixture = mixed * inverse
    delta = jnp.sum(d_out * mixture, axis=1, keepdims=True)
    shift = -delta * inverse
    coarse = shift.astype(BF16).astype(F32)
    scaled = jnp.where(lane == HS, coarse, jnp.where(lane == HS + 1, shift - coarse, d_out * inverse))
    return mixture, scaled.astype(BF16)


def work_kernel(reach, tok_rows, max_tiles, table, *refs):
    count = 2 * reach + 1
    inputs, outputs = refs[:count], refs[count : 2 * count]
    x, y, qb, kb, vb, db, eb, dk, dv, in_sem, out_sem = refs[2 * count :]

    def copy_in(b):
        return pltpu.make_async_copy(inputs[b], x.at[pl.ds(b * tok_rows, tok_rows)], in_sem.at[b])

    def copy_out(b):
        return pltpu.make_async_copy(y.at[pl.ds(b * tok_rows, tok_rows)], outputs[b], out_sem.at[b])

    for b in range(count):
        copy_in(b).start()
    for b in range(count):
        copy_in(b).wait()
    row = lax.broadcasted_iota(jnp.int32, (TILE, 128), 0)
    lane = lax.broadcasted_iota(jnp.int32, (TILE, 128), 1)
    low = lane < HS

    @pl.loop(0, 2 * reach)
    def _(job):
        length = table[4 + 2 * reach + job]
        first = table[4 + job]
        aligned = pl.multiple_of((first // 16) * 16, 16)
        lead = first - aligned
        tiles = (lead + length + TILE - 1) // TILE
        tiles = jnp.where(length > 0, tiles, 0)

        def inside(t):
            at = row + t * TILE
            return (at >= lead) & (at < lead + length)

        @pl.loop(0, tiles)
        def _(t):
            at = pl.multiple_of(t * TILE, TILE)
            source = pl.ds(aligned + at, TILE)
            ours = inside(t)
            keep = low & ours
            qk = x[source, 0:128].astype(F32)
            vd = x[source, 128:256].astype(F32)
            ones = jnp.where(lane < HS + 2, 1.0, 0.0)
            qb[pl.ds(at, TILE), :] = jnp.where(keep, qk, 0.0).astype(BF16)
            kb[pl.ds(at, TILE), :] = jnp.where(keep, pltpu.roll(qk, HS, 1), 0.0).astype(BF16)
            vb[pl.ds(at, TILE), :] = jnp.where(ours, jnp.where(low, vd, ones), 0.0).astype(BF16)
            db[pl.ds(at, TILE), :] = jnp.where(keep, pltpu.roll(vd, HS, 1), 0.0).astype(BF16)
            dk[:, pl.ds(at, TILE)] = jnp.zeros((HS, TILE), F32)
            dv[:, pl.ds(at, TILE)] = jnp.zeros((HS, TILE), F32)

        def store(t, lanes, value):
            place = pl.ds(aligned + pl.multiple_of(t * TILE, TILE), TILE)
            old = y[place, lanes].astype(F32)
            y[place, lanes] = jnp.where(inside(t), value, old).astype(BF16)

        def first_pass(q, at):
            e = jnp.exp(dot_nt(q, kb[at, :])).astype(BF16)
            eb[:, at] = e

        def second_pass(q, scaled, at):
            e = eb[:, at]
            dv[:, at] += dot_tn(scaled[:, :HS], e)
            grad = dot_nt(scaled, vb[at, :])
            ds = (e.astype(F32) * grad).astype(BF16)
            eb[:, at] = ds
            dk[:, at] += dot_tn(q[:, :HS], ds)

        @pl.when(tiles == max_tiles)
        def _():
            @pl.loop(0, max_tiles)
            def _(t):
                at = pl.ds(pl.multiple_of(t * TILE, TILE), TILE)
                q = qb[at, :]
                for s in range(max_tiles):
                    first_pass(q, slice(s * TILE, (s + 1) * TILE))
                mixture, scaled = softmax_tail(dot_nn(eb[...], vb[...]), db[at, :].astype(F32))
                for s in range(max_tiles):
                    second_pass(q, scaled, slice(s * TILE, (s + 1) * TILE))
                d_query = dot_nn(eb[...], kb[...])
                store(t, slice(0, 128), jnp.where(low, mixture, pltpu.roll(d_query, HS, 1)))

        @pl.when((tiles > 0) & (tiles < max_tiles))
        def _():
            @pl.loop(0, tiles)
            def _(t):
                at = pl.ds(pl.multiple_of(t * TILE, TILE), TILE)
                q = qb[at, :]

                def mix(s, total):
                    to = pl.ds(pl.multiple_of(s * TILE, TILE), TILE)
                    first_pass(q, to)
                    return total + dot_nn(eb[:, to], vb[to, :])

                mixed = lax.fori_loop(0, tiles, mix, jnp.zeros((TILE, 128), F32))
                mixture, scaled = softmax_tail(mixed, db[at, :].astype(F32))

                def back(s, total):
                    to = pl.ds(pl.multiple_of(s * TILE, TILE), TILE)
                    second_pass(q, scaled, to)
                    return total + dot_nn(eb[:, to], kb[to, :])

                d_query = lax.fori_loop(0, tiles, back, jnp.zeros((TILE, 128), F32))
                store(t, slice(0, 128), jnp.where(low, mixture, pltpu.roll(d_query, HS, 1)))

        @pl.loop(0, tiles)
        def _(t):
            at = pl.ds(pl.multiple_of(t * TILE, TILE), TILE)
            both = jnp.concatenate([dk[:, at], dv[:, at]], axis=0)
            store(t, slice(128, 256), both.T)

    for b in range(count):
        copy_out(b).start()
    for b in range(count):
        copy_out(b).wait()


def local_kernel(heads, table, local, ids_row, ids_column, out):
    rows = local.shape[1]

    @pl.when(table[0] < table[1])
    def _():
        lane = lax.broadcasted_iota(jnp.int32, (rows, 128), 1)
        low = lane < HS
        same = (ids_column[...] == ids_row[...]).astype(F32)
        ones = jnp.where(lane < HS + 2, 1.0, 0.0)

        @pl.loop(0, heads)
        def _(h):
            qk = local[h, :, 0:128].astype(F32)
            vd = local[h, :, 128:256].astype(F32)
            q = jnp.where(low, qk, 0.0).astype(BF16)
            k = jnp.where(low, pltpu.roll(qk, HS, 1), 0.0).astype(BF16)
            v = jnp.where(low, vd, ones).astype(BF16)
            d_out = jnp.where(low, pltpu.roll(vd, HS, 1), 0.0)
            e = (jnp.exp(dot_nt(q, k)) * same).astype(BF16)
            mixture, scaled = softmax_tail(dot_nn(e, v), d_out)
            ds = (e.astype(F32) * dot_nt(scaled, v)).astype(BF16)
            d_query = dot_nn(ds, k)
            d_key = dot_tn(q[:, :HS], ds)
            d_value = dot_tn(scaled[:, :HS], e)
            out[h, :, 0:128] = jnp.where(low, mixture, pltpu.roll(d_query, HS, 1)).astype(BF16)
            out[h, :, 128:256] = jnp.concatenate([d_key, d_value], axis=0).T.astype(BF16)


def unpack_kernel(heads, reach, table, proj, gains, local, *refs):
    count = 2 * reach + 1
    backs = refs[:count]
    attended, d_proj, gain_sums, stacked, sems = refs[count:]
    rows = proj.shape[1]

    def copy_in(b):
        return pltpu.make_async_copy(backs[b], stacked.at[b], sems.at[b])

    for b in range(count):
        copy_in(b).start()
    for b in range(count):
        copy_in(b).wait()
    low = lax.broadcasted_iota(jnp.int32, (rows, 128), 1) < HS
    row = lax.broadcasted_iota(jnp.int32, (rows, 256), 0)
    from_low = row < table[0]
    from_high = row >= table[1]
    q_gain = gains[0:1, :] * (HS**-0.5)
    k_gain = gains[1:2, :]

    def gathered(h):
        lower = stacked[h - table[2] + reach].astype(F32)
        upper = stacked[h - table[3] + reach].astype(F32)
        return jnp.where(from_low, lower, jnp.where(from_high, upper, local[h].astype(F32)))

    def back(raw, gradient, gain):
        hat, inverse = normalized_halves(raw)
        scaled = gradient * gain
        shifted = scaled - half_means(scaled) - hat * half_means(scaled * hat)
        return shifted * inverse, jnp.sum(gradient * hat, axis=0, keepdims=True)

    q_sum = jnp.zeros((1, 128), F32)
    k_sum = jnp.zeros((1, 128), F32)
    for pair in range(heads // 2):
        lanes = slice(pair * 128, (pair + 1) * 128)
        even, odd = gathered(2 * pair), gathered(2 * pair + 1)
        mixture = jnp.where(low, even[:, 0:128], pltpu.roll(odd[:, 0:128], HS, 1))
        d_query = jnp.where(low, pltpu.roll(even[:, 0:128], HS, 1), odd[:, 0:128])
        d_key = jnp.where(low, even[:, 128:256], pltpu.roll(odd[:, 128:256], HS, 1))
        d_value = jnp.where(low, pltpu.roll(even[:, 128:256], HS, 1), odd[:, 128:256])
        attended[:, lanes] = mixture.astype(BF16)
        q_raw, q_part = back(proj[0, :, lanes], d_query, q_gain)
        k_raw, k_part = back(proj[1, :, lanes], d_key, k_gain)
        q_sum += q_part
        k_sum += k_part
        d_proj[0, :, lanes] = q_raw.astype(BF16)
        d_proj[1, :, lanes] = k_raw.astype(BF16)
        d_proj[2, :, lanes] = d_value.astype(BF16)
    gain_sums[...] = jnp.concatenate([q_sum * (HS**-0.5), k_sum], axis=0)


def in_vmem():
    return pl.BlockSpec(memory_space=pltpu.VMEM)


def in_smem():
    return pl.BlockSpec(memory_space=pltpu.SMEM)


def anywhere():
    return pl.BlockSpec(memory_space=pl.ANY)


def compiler_params():
    return pltpu.CompilerParams(vmem_limit_bytes=VMEM_LIMIT)


def cost(flops, bytes_accessed, transcendentals=0):
    return pl.CostEstimate(
        flops=flops, bytes_accessed=bytes_accessed, transcendentals=transcendentals
    )


def pack(heads, reach, table, proj, datt, gains):
    rows = proj.shape[1]
    slot = jax.ShapeDtypeStruct((rows, 4 * HS), BF16)
    count = 2 * reach + 1
    return pl.pallas_call(
        functools.partial(pack_kernel, heads, reach),
        out_shape=[slot] * count + [jax.ShapeDtypeStruct((heads, rows, 4 * HS), BF16)],
        in_specs=[in_smem(), in_vmem(), in_vmem(), in_vmem()],
        out_specs=[in_vmem()] * (count + 1),
        compiler_params=compiler_params(),
        cost_estimate=cost(10**9, 10**7),
    )(table, proj, datt, gains)


def work(reach, tok_rows, table, blocks):
    count = 2 * reach + 1
    max_tiles = -(-(LONG_LEN + 15) // TILE)
    padded = count * tok_rows + TILE
    span = max_tiles * TILE
    return pl.pallas_call(
        functools.partial(work_kernel, reach, tok_rows, max_tiles),
        out_shape=[jax.ShapeDtypeStruct((tok_rows, 4 * HS), BF16)] * count,
        in_specs=[in_smem()] + [anywhere()] * count,
        out_specs=[anywhere()] * count,
        scratch_shapes=[
            pltpu.VMEM((padded, 4 * HS), BF16),
            pltpu.VMEM((padded, 4 * HS), BF16),
            pltpu.VMEM((span, 128), BF16),
            pltpu.VMEM((span, 128), BF16),
            pltpu.VMEM((span, 128), BF16),
            pltpu.VMEM((span, 128), BF16),
            pltpu.VMEM((TILE, span), BF16),
            pltpu.VMEM((HS, span), F32),
            pltpu.VMEM((HS, span), F32),
            pltpu.SemaphoreType.DMA((count,)),
            pltpu.SemaphoreType.DMA((count,)),
        ],
        compiler_params=compiler_params(),
        cost_estimate=cost(3 * 10**10, 10**7, 10**7),
    )(table, *blocks)


def local_work(heads, table, local, ids_row, ids_column):
    return pl.pallas_call(
        functools.partial(local_kernel, heads),
        out_shape=jax.ShapeDtypeStruct(local.shape, BF16),
        in_specs=[in_smem(), in_vmem(), in_vmem(), in_vmem()],
        out_specs=in_vmem(),
        compiler_params=compiler_params(),
        cost_estimate=cost(5 * 10**9, 4 * 10**6, 25 * 10**5),
    )(table, local, ids_row, ids_column)


def unpack(heads, reach, table, proj, gains, local, backs):
    rows = proj.shape[1]
    count = 2 * reach + 1
    width = heads * HS
    return pl.pallas_call(
        functools.partial(unpack_kernel, heads, reach),
        out_shape=[
            jax.ShapeDtypeStruct((rows, width), BF16),
            jax.ShapeDtypeStruct((3, rows, width), BF16),
            jax.ShapeDtypeStruct((2, 128), F32),
        ],
        in_specs=[in_smem(), in_vmem(), in_vmem(), in_vmem()] + [anywhere()] * count,
        out_specs=[in_vmem()] * 3,
        scratch_shapes=[
            pltpu.VMEM((count, rows, 4 * HS), BF16),
            pltpu.SemaphoreType.DMA((count,)),
        ],
        compiler_params=compiler_params(),
        cost_estimate=cost(10**9, 10**7),
    )(table, proj, gains, local, *backs)


def on_device(
    tokens,
    image_starts,
    ln_gain,
    w_qkv,
    q_gain,
    k_gain,
    w_up,
    up_bias,
    w_attn_out,
    w_down,
    out_bias,
    cotangent,
):
    tok_rows, half = tokens.shape
    local_width = w_qkv.shape[2]
    heads = local_width // HS
    reach = (LONG_LEN + tok_rows - 2) // tok_rows
    n_seq = lax.axis_size("seq")
    place = lax.axis_index("seq")
    side = lax.axis_index("head")
    assert heads == reach + 1 and n_seq >= heads and heads % 2 == 0

    def from_peer(block):
        return lax.ppermute(block, "head", [(0, 1), (1, 0)])

    def both_halves(block):
        other = from_peer(block)
        first = jnp.where(side == 0, block, other)
        second = jnp.where(side == 0, other, block)
        return jnp.concatenate([first, second], axis=1)

    def add_over_heads(partial):
        low, high = partial[:, :half], partial[:, half:]
        send = jnp.where(side == 0, high, low).astype(BF16)
        keep = jnp.where(side == 0, low, high)
        return keep + from_peer(send).astype(F32)

    def shifted(block, distance):
        if distance == 0:
            return block
        route = [(i, i + distance) for i in range(n_seq) if 0 <= i + distance < n_seq]
        return lax.ppermute(block, "seq", route)

    table = work_table(image_starts, place, n_seq, tok_rows, reach)
    row_index = jnp.arange(tok_rows, dtype=jnp.int32)
    positions = place * tok_rows + row_index
    ids = jnp.sum((image_starts[None, :] <= positions[:, None]).astype(jnp.int32), axis=1)
    is_local = (row_index >= table[0]) & (row_index < table[1])
    ids_column = jnp.where(is_local, ids, -1)[:, None]
    ids_row = jnp.where(is_local, ids, -2)[None, :]
    gains = jnp.tile(jnp.stack([q_gain, k_gain]), (1, 2))

    gathered = both_halves(tokens)
    cot_whole = both_halves(cotangent)
    normed_f, norm_pull = jax.vjp(layer_norm, gathered.astype(F32), ln_gain)
    normed = normed_f.astype(BF16)
    proj = jnp.einsum("td,dkc->ktc", normed, w_qkv, preferred_element_type=F32)
    d_attended = jnp.einsum("td,cd->tc", cot_whole, w_attn_out, preferred_element_type=F32)
    packed = pack(heads, reach, table, proj, d_attended.astype(BF16), gains)
    slots, local = packed[:-1], packed[-1]

    arrived = [shifted(slots[reach + d], d) for d in range(reach, -reach - 1, -1)]

    up_input = jnp.dot(normed, w_up, preferred_element_type=F32) + up_bias
    hidden_f, gelu_pull = jax.vjp(exact_gelu, up_input)
    hidden = hidden_f.astype(BF16)
    d_hidden = jnp.einsum("td,fd->tf", cot_whole, w_down, preferred_element_type=F32)
    d_upper_f = gelu_pull(d_hidden)[0]
    d_upper = d_upper_f.astype(BF16)
    grad_down = jnp.einsum("tf,td->fd", hidden, cot_whole, preferred_element_type=F32)
    grad_up = jnp.einsum("td,tf->df", normed, d_upper, preferred_element_type=F32)
    grad_out_bias = jnp.sum(cotangent.astype(F32), axis=0)
    grad_up_bias = jnp.sum(d_upper.astype(F32), axis=0)
    early = lax.psum((grad_down.astype(BF16), grad_up.astype(BF16)), "seq")
    ffn_out = jnp.dot(hidden, w_down, preferred_element_type=F32)
    ffn_back = jnp.einsum("tf,df->td", d_upper, w_up, preferred_element_type=F32)

    local_out = local_work(heads, table, local, ids_row, ids_column)
    worked = work(reach, tok_rows, table, arrived)
    returned = [shifted(worked[b], b - reach) for b in range(2 * reach + 1)][::-1]
    attended, d_proj, gain_sums = unpack(heads, reach, table, proj, gains, local_out, returned)

    partial_out = jnp.dot(attended, w_attn_out, preferred_element_type=F32) + ffn_out
    summed = add_over_heads(partial_out)
    block_out = (summed + tokens.astype(F32) + out_bias).astype(BF16)
    grad_attn_out = jnp.einsum("tc,td->cd", attended, cot_whole, preferred_element_type=F32)
    grad_qkv = jnp.einsum("td,ktc->dkc", normed, d_proj, preferred_element_type=F32)
    d_normed = ffn_back + jnp.einsum("ktc,dkc->td", d_proj, w_qkv, preferred_element_type=F32)
    d_input, d_ln = norm_pull(d_normed)
    input_sum = add_over_heads(d_input)
    tokens_grad = (input_sum + cotangent.astype(F32)).astype(BF16)
    gain_total = gain_sums[:, :HS] + gain_sums[:, HS:]
    small = jnp.concatenate([d_ln, gain_total.reshape(-1), grad_up_bias, grad_out_bias])
    parts = (grad_qkv.astype(BF16), grad_attn_out.astype(BF16), small[None].astype(BF16))
    parts, early = lax.optimization_barrier((parts, early))
    late = lax.psum(parts, "seq")
    sums = late[2][0].astype(F32)
    width = 2 * half
    shared = add_over_heads(sums[None, :width])[0]
    gain_pair = sums[width : width + 2 * HS].reshape(2, HS)
    gain_half = HS // 2
    gain_send = jnp.where(side == 0, gain_pair[:, gain_half:], gain_pair[:, :gain_half])
    gain_keep = jnp.where(side == 0, gain_pair[:, :gain_half], gain_pair[:, gain_half:])
    gain_grads = gain_keep + from_peer(gain_send)
    at = width + 2 * HS
    up_width = up_bias.shape[0]
    return (
        block_out,
        tokens_grad,
        shared,
        late[0].astype(F32),
        gain_grads[0],
        gain_grads[1],
        early[1].astype(F32),
        sums[at : at + up_width],
        late[1].astype(F32),
        early[0].astype(F32),
        sums[at + up_width :],
    )


def solution(mesh):
    in_specs = (
        P("seq", "head"),
        P(),
        P(),
        P(None, None, "head"),
        P(),
        P(),
        P(None, "head"),
        P("head"),
        P("head", None),
        P("head", None),
        P("head"),
        P("seq", "head"),
    )
    out_specs = (
        P("seq", "head"),
        P("seq", "head"),
        P("head"),
        P(None, None, "head"),
        P("head"),
        P("head"),
        P(None, "head"),
        P("head"),
        P("head", None),
        P("head", None),
        P("head"),
    )
    return jax.shard_map(
        on_device, mesh=mesh, in_specs=in_specs, out_specs=out_specs, check_vma=False
    )
```

```python
import functools

import jax
import jax.numpy as jnp
from jax import lax
from jax.experimental import pallas as pl
from jax.experimental.pallas import tpu as pltpu
from jax.sharding import PartitionSpec as P

HS = 64
LONG_LEN = 3136
EPSILON = 1e-06
F32 = jnp.float32
BF16 = jnp.bfloat16
TILE = 256
GROUP = 4
VMEM_LIMIT = 60 * 1024 * 1024


def layer_norm(values, gain_row):
    row_mean = jnp.mean(values, axis=-1, keepdims=True)
    centred = values - row_mean
    spread = jnp.mean(centred * centred, axis=-1, keepdims=True)
    return centred * lax.rsqrt(spread + EPSILON) * gain_row


def exact_gelu(values):
    return jax.nn.gelu(values, approximate=False)


def dot_nn(a, b):
    return lax.dot_general(a, b, (((1,), (0,)), ((), ())), preferred_element_type=F32)


def dot_nt(a, b):
    return lax.dot_general(a, b, (((1,), (1,)), ((), ())), preferred_element_type=F32)


def dot_tn(a, b):
    return lax.dot_general(a, b, (((0,), (0,)), ((), ())), preferred_element_type=F32)


def half_means(block):
    left = (lax.broadcasted_iota(jnp.int32, (256, 128), 0) % 128) // HS
    right = lax.broadcasted_iota(jnp.int32, (256, 128), 1) // HS
    averager = jnp.where(left == right, 1.0 / HS, 0.0).astype(BF16)
    coarse = block.astype(BF16)
    fine = (block - coarse.astype(F32)).astype(BF16)
    return dot_nn(jnp.concatenate([coarse, fine], axis=1), averager)


def normalized_halves(block):
    centred = block - half_means(block)
    inverse = lax.rsqrt(half_means(centred * centred) + EPSILON)
    return centred * inverse, inverse


def work_table(image_starts, place, n_seq, tok_rows, reach):
    window = reach + 1
    total = n_seq * tok_rows
    candidates = jnp.arange(2 * reach, dtype=jnp.int32) + place - reach
    positions = jnp.concatenate(
        [(candidates + 1) * tok_rows - 1, jnp.stack([place * tok_rows, (place + 1) * tok_rows - 1])]
    )
    below = image_starts[None, :] <= positions[:, None]
    starts = jnp.max(jnp.where(below, image_starts[None, :], -1), axis=1)
    ends = jnp.min(jnp.where(below, total, image_starts[None, :]), axis=1)
    first = starts // tok_rows
    last = (ends - 1) // tok_rows
    base = jnp.minimum(first, n_seq - window)
    spans = last > first
    mine = (
        (candidates >= 0)
        & (candidates < n_seq)
        & (first[:-2] == candidates)
        & spans[:-2]
        & (base[:-2] <= place)
        & (base[:-2] >= place - reach)
    )
    lengths = jnp.where(mine, ends[:-2] - starts[:-2], 0)
    rows = jnp.where(mine, starts[:-2] - (place - reach) * tok_rows, 0)
    low_end = jnp.where(spans[-2], jnp.clip(ends[-2] - place * tok_rows, 0, tok_rows), 0)
    low_end = jnp.where(first[-2] < place, low_end, 0)
    high_start = jnp.clip(starts[-1] - place * tok_rows, 0, tok_rows)
    high_start = jnp.where(last[-1] > place, high_start, tok_rows)
    head_part = jnp.stack([low_end, high_start, place - base[-2], place - base[-1]])
    return jnp.concatenate([head_part, rows, lengths]).astype(jnp.int32)


def pack_kernel(heads, reach, table, proj, datt, gains, *outs):
    slots, local = outs[:-1], outs[-1]
    rows = proj.shape[1]
    low = lax.broadcasted_iota(jnp.int32, (rows, 128), 1) < HS
    q_gain = gains[0:1, :] * (HS**-0.5)
    k_gain = gains[1:2, :]
    for pair in range(heads // 2):
        lanes = slice(pair * 128, (pair + 1) * 128)
        q = normalized_halves(proj[0, :, lanes])[0] * q_gain
        k = normalized_halves(proj[1, :, lanes])[0] * k_gain
        v = proj[2, :, lanes]
        d = datt[:, lanes].astype(F32)
        q, k, v = (t.astype(BF16).astype(F32) for t in (q, k, v))
        local[2 * pair, :, 0:128] = jnp.where(low, q, pltpu.roll(k, HS, 1)).astype(BF16)
        local[2 * pair, :, 128:256] = jnp.where(low, v, pltpu.roll(d, HS, 1)).astype(BF16)
        local[2 * pair + 1, :, 0:128] = jnp.where(low, pltpu.roll(q, HS, 1), k).astype(BF16)
        local[2 * pair + 1, :, 128:256] = jnp.where(low, pltpu.roll(v, HS, 1), d).astype(BF16)
    low_end = table[0]
    from_low = lax.broadcasted_iota(jnp.int32, (rows, 256), 0) < low_end
    for index, slot in enumerate(slots):
        distance = index - reach
        low_head = jnp.clip(table[2] + distance, 0, heads - 1)
        high_head = jnp.clip(table[3] + distance, 0, heads - 1)
        picked = jnp.where(from_low, local[low_head].astype(F32), local[high_head].astype(F32))
        slot[...] = picked.astype(BF16)


def softmax_tail(mixed, d_out):
    lane = lax.broadcasted_iota(jnp.int32, mixed.shape, 1)
    total = mixed[:, HS : HS + 1]
    inverse = 1.0 / jnp.where(total > 0, total, 1.0)
    mixture = mixed * inverse
    delta = jnp.sum(d_out * mixture, axis=1, keepdims=True)
    shift = -delta * inverse
    coarse = shift.astype(BF16).astype(F32)
    scaled = jnp.where(lane == HS, coarse, jnp.where(lane == HS + 1, shift - coarse, d_out * inverse))
    return mixture, scaled.astype(BF16)


def work_kernel(reach, tok_rows, max_tiles, table, *refs):
    count = 2 * reach + 1
    inputs, outputs = refs[:count], refs[count : 2 * count]
    x, y, qb, kb, vb, db, eb, dk, dv, in_sem, out_sem = refs[2 * count :]

    def copy_in(b):
        return pltpu.make_async_copy(inputs[b], x.at[pl.ds(b * tok_rows, tok_rows)], in_sem.at[b])

    def copy_out(b):
        return pltpu.make_async_copy(y.at[pl.ds(b * tok_rows, tok_rows)], outputs[b], out_sem.at[b])

    for b in range(count):
        copy_in(b).start()
    for b in range(count):
        copy_in(b).wait()
    row = lax.broadcasted_iota(jnp.int32, (TILE, 128), 0)
    lane = lax.broadcasted_iota(jnp.int32, (TILE, 128), 1)
    low = lane < HS

    @pl.loop(0, 2 * reach)
    def _(job):
        length = table[4 + 2 * reach + job]
        first = table[4 + job]
        aligned = pl.multiple_of((first // 16) * 16, 16)
        lead = first - aligned
        tiles = (lead + length + TILE - 1) // TILE
        tiles = jnp.where(length > 0, tiles, 0)
        groups = (tiles + GROUP - 1) // GROUP
        grouped = (tiles > 2) & (tiles < max_tiles)
        prepared = jnp.where(grouped, groups * GROUP, tiles)

        def inside(t):
            at = row + t * TILE
            return (at >= lead) & (at < lead + length)

        @pl.loop(0, prepared)
        def _(t):
            at = pl.multiple_of(t * TILE, TILE)
            source = pl.ds(aligned + at, TILE)
            ours = inside(t)
            keep = low & ours
            qk = x[source, 0:128].astype(F32)
            vd = x[source, 128:256].astype(F32)
            ones = jnp.where(lane < HS + 2, 1.0, 0.0)
            qb[pl.ds(at, TILE), :] = jnp.where(keep, qk, 0.0).astype(BF16)
            kb[pl.ds(at, TILE), :] = jnp.where(keep, pltpu.roll(qk, HS, 1), 0.0).astype(BF16)
            vb[pl.ds(at, TILE), :] = jnp.where(ours, jnp.where(low, vd, ones), 0.0).astype(BF16)
            db[pl.ds(at, TILE), :] = jnp.where(keep, pltpu.roll(vd, HS, 1), 0.0).astype(BF16)
            dk[:, pl.ds(at, TILE)] = jnp.zeros((HS, TILE), F32)
            dv[:, pl.ds(at, TILE)] = jnp.zeros((HS, TILE), F32)

        def store(t, lanes, value):
            place = pl.ds(aligned + pl.multiple_of(t * TILE, TILE), TILE)
            old = y[place, lanes].astype(F32)
            y[place, lanes] = jnp.where(inside(t), value, old).astype(BF16)

        def first_pass(q, at):
            e = jnp.exp(dot_nt(q, kb[at, :])).astype(BF16)
            eb[:, at] = e

        def second_pass(q, scaled, at):
            e = eb[:, at]
            dv[:, at] += dot_tn(scaled[:, :HS], e)
            grad = dot_nt(scaled, vb[at, :])
            ds = (e.astype(F32) * grad).astype(BF16)
            eb[:, at] = ds
            dk[:, at] += dot_tn(q[:, :HS], ds)

        @pl.when(tiles == max_tiles)
        def _():
            @pl.loop(0, max_tiles)
            def _(t):
                at = pl.ds(pl.multiple_of(t * TILE, TILE), TILE)
                q = qb[at, :]
                for s in range(max_tiles):
                    first_pass(q, slice(s * TILE, (s + 1) * TILE))
                mixture, scaled = softmax_tail(dot_nn(eb[...], vb[...]), db[at, :].astype(F32))
                for s in range(max_tiles):
                    second_pass(q, scaled, slice(s * TILE, (s + 1) * TILE))
                d_query = dot_nn(eb[...], kb[...])
                store(t, slice(0, 128), jnp.where(low, mixture, pltpu.roll(d_query, HS, 1)))

        @pl.when(grouped)
        def _():
            @pl.loop(0, tiles)
            def _(t):
                at = pl.ds(pl.multiple_of(t * TILE, TILE), TILE)
                q = qb[at, :]

                def mix(g, total):
                    for s in range(GROUP):
                        first_pass(q, pl.ds(pl.multiple_of((g * GROUP + s) * TILE, TILE), TILE))
                    to = pl.ds(pl.multiple_of(g * GROUP * TILE, GROUP * TILE), GROUP * TILE)
                    return total + dot_nn(eb[:, to], vb[to, :])

                mixed = lax.fori_loop(0, groups, mix, jnp.zeros((TILE, 128), F32))
                mixture, scaled = softmax_tail(mixed, db[at, :].astype(F32))

                def back(g, total):
                    for s in range(GROUP):
                        to = pl.ds(pl.multiple_of((g * GROUP + s) * TILE, TILE), TILE)
                        second_pass(q, scaled, to)
                    to = pl.ds(pl.multiple_of(g * GROUP * TILE, GROUP * TILE), GROUP * TILE)
                    return total + dot_nn(eb[:, to], kb[to, :])

                d_query = lax.fori_loop(0, groups, back, jnp.zeros((TILE, 128), F32))
                store(t, slice(0, 128), jnp.where(low, mixture, pltpu.roll(d_query, HS, 1)))

        @pl.when((tiles > 0) & (tiles <= 2))
        def _():
            @pl.loop(0, tiles)
            def _(t):
                at = pl.ds(pl.multiple_of(t * TILE, TILE), TILE)
                q = qb[at, :]

                def mix(s, total):
                    to = pl.ds(pl.multiple_of(s * TILE, TILE), TILE)
                    first_pass(q, to)
                    return total + dot_nn(eb[:, to], vb[to, :])

                mixed = lax.fori_loop(0, tiles, mix, jnp.zeros((TILE, 128), F32))
                mixture, scaled = softmax_tail(mixed, db[at, :].astype(F32))

                def back(s, total):
                    to = pl.ds(pl.multiple_of(s * TILE, TILE), TILE)
                    second_pass(q, scaled, to)
                    return total + dot_nn(eb[:, to], kb[to, :])

                d_query = lax.fori_loop(0, tiles, back, jnp.zeros((TILE, 128), F32))
                store(t, slice(0, 128), jnp.where(low, mixture, pltpu.roll(d_query, HS, 1)))

        @pl.loop(0, tiles)
        def _(t):
            at = pl.ds(pl.multiple_of(t * TILE, TILE), TILE)
            both = jnp.concatenate([dk[:, at], dv[:, at]], axis=0)
            store(t, slice(128, 256), both.T)

    for b in range(count):
        copy_out(b).start()
    for b in range(count):
        copy_out(b).wait()


def local_kernel(heads, table, local, ids_row, ids_column, out):
    rows = local.shape[1]

    @pl.when(table[0] < table[1])
    def _():
        lane = lax.broadcasted_iota(jnp.int32, (rows, 128), 1)
        low = lane < HS
        same = (ids_column[...] == ids_row[...]).astype(F32)
        ones = jnp.where(lane < HS + 2, 1.0, 0.0)

        @pl.loop(0, heads)
        def _(h):
            qk = local[h, :, 0:128].astype(F32)
            vd = local[h, :, 128:256].astype(F32)
            q = jnp.where(low, qk, 0.0).astype(BF16)
            k = jnp.where(low, pltpu.roll(qk, HS, 1), 0.0).astype(BF16)
            v = jnp.where(low, vd, ones).astype(BF16)
            d_out = jnp.where(low, pltpu.roll(vd, HS, 1), 0.0)
            e = (jnp.exp(dot_nt(q, k)) * same).astype(BF16)
            mixture, scaled = softmax_tail(dot_nn(e, v), d_out)
            ds = (e.astype(F32) * dot_nt(scaled, v)).astype(BF16)
            d_query = dot_nn(ds, k)
            d_key = dot_tn(q[:, :HS], ds)
            d_value = dot_tn(scaled[:, :HS], e)
            out[h, :, 0:128] = jnp.where(low, mixture, pltpu.roll(d_query, HS, 1)).astype(BF16)
            out[h, :, 128:256] = jnp.concatenate([d_key, d_value], axis=0).T.astype(BF16)


def unpack_kernel(heads, reach, table, proj, gains, local, normed, cot, *refs):
    count = 2 * reach + 1
    backs = refs[:count]
    attended, d_proj, gain_sums, grads, stacked, sems = refs[count:]
    rows = proj.shape[1]

    def copy_in(b):
        return pltpu.make_async_copy(backs[b], stacked.at[b], sems.at[b])

    for b in range(count):
        copy_in(b).start()
    for b in range(count):
        copy_in(b).wait()
    low = lax.broadcasted_iota(jnp.int32, (rows, 128), 1) < HS
    row = lax.broadcasted_iota(jnp.int32, (rows, 256), 0)
    from_low = row < table[0]
    from_high = row >= table[1]
    q_gain = gains[0:1, :] * (HS**-0.5)
    k_gain = gains[1:2, :]

    def gathered(h):
        lower = stacked[h - table[2] + reach].astype(F32)
        upper = stacked[h - table[3] + reach].astype(F32)
        return jnp.where(from_low, lower, jnp.where(from_high, upper, local[h].astype(F32)))

    def back(raw, gradient, gain):
        hat, inverse = normalized_halves(raw)
        scaled = gradient * gain
        shifted = scaled - half_means(scaled) - hat * half_means(scaled * hat)
        return shifted * inverse, jnp.sum(gradient * hat, axis=0, keepdims=True)

    q_sum = jnp.zeros((1, 128), F32)
    k_sum = jnp.zeros((1, 128), F32)
    for pair in range(heads // 2):
        lanes = slice(pair * 128, (pair + 1) * 128)
        even, odd = gathered(2 * pair), gathered(2 * pair + 1)
        mixture = jnp.where(low, even[:, 0:128], pltpu.roll(odd[:, 0:128], HS, 1))
        d_query = jnp.where(low, pltpu.roll(even[:, 0:128], HS, 1), odd[:, 0:128])
        d_key = jnp.where(low, even[:, 128:256], pltpu.roll(odd[:, 128:256], HS, 1))
        d_value = jnp.where(low, pltpu.roll(even[:, 128:256], HS, 1), odd[:, 128:256])
        attended[:, lanes] = mixture.astype(BF16)
        q_raw, q_part = back(proj[0, :, lanes], d_query, q_gain)
        k_raw, k_part = back(proj[1, :, lanes], d_key, k_gain)
        q_sum += q_part
        k_sum += k_part
        d_proj[0, :, lanes] = q_raw.astype(BF16)
        d_proj[1, :, lanes] = k_raw.astype(BF16)
        d_proj[2, :, lanes] = d_value.astype(BF16)
    gain_sums[...] = jnp.concatenate([q_sum * (HS**-0.5), k_sum], axis=0)
    width, columns = normed.shape[1], heads * HS
    for part in range(3):
        grads[part * width : (part + 1) * width, :] = dot_tn(normed[...], d_proj[part]).astype(BF16)
    for part in range(width // columns):
        at = 3 * width + part * columns
        lanes = slice(part * columns, (part + 1) * columns)
        grads[at : at + columns, :] = dot_tn(attended[...], cot[:, lanes]).astype(BF16)


class SeqSum:
    def __init__(self, blocks, place, n_seq, small=None):
        width = n_seq.bit_length() - 1
        self.n_seq = n_seq
        stages = [(bit, 1 << min(2, width - bit)) for bit in range(0, width, 2)]
        self.order = stages + stages[::-1]
        self.phases = len(self.order)
        self.codes = {bit: (place >> bit) & (radix - 1) for bit, radix in stages}
        self.current, self.small = blocks, small

    def describe(self, phase):
        bit, radix = self.order[phase]
        adding = phase < self.phases // 2
        joins = self.small is not None and adding == (bit > 0)
        return bit, radix, adding, joins, self.codes[bit]

    def split(self, radix):
        rows, lanes = self.current.shape
        return self.current.reshape(radix, rows // radix, lanes)

    def send(self, phase):
        bit, radix, adding, joins, code = self.describe(phase)
        tail = self.small.astype(BF16) if joins else None
        arrived = []
        for mask in reversed(range(1, radix)):
            block = self.current
            if adding:
                block = lax.dynamic_index_in_dim(self.split(radix), code ^ mask, 0, keepdims=False)
            if joins:
                block = jnp.concatenate([block, tail], axis=0)
            route = [(i, i ^ (mask << bit)) for i in range(self.n_seq)]
            arrived.append(lax.ppermute(block, "seq", route))
        return arrived

    def receive(self, phase, arrived):
        bit, radix, adding, joins, code = self.describe(phase)
        rows, lanes = self.current.shape
        height = rows // radix if adding else rows
        if adding:
            total = lax.dynamic_index_in_dim(self.split(radix), code, 0, keepdims=False).astype(F32)
            for block in arrived:
                total = total + block[:height].astype(F32)
            self.current = total.astype(BF16)
        else:
            whole = jnp.zeros((radix, height, lanes), BF16)
            whole = lax.dynamic_update_index_in_dim(whole, self.current, code, 0)
            for mask, block in zip(reversed(range(1, radix)), arrived):
                whole = lax.dynamic_update_index_in_dim(whole, block[:height], code ^ mask, 0)
            self.current = whole.reshape(radix * height, lanes)
        if joins:
            small = self.small.astype(BF16).astype(F32)
            for block in arrived:
                small = small + block[height:].astype(F32)
            self.small = small


def in_vmem():
    return pl.BlockSpec(memory_space=pltpu.VMEM)


def in_smem():
    return pl.BlockSpec(memory_space=pltpu.SMEM)


def anywhere():
    return pl.BlockSpec(memory_space=pl.ANY)


def compiler_params():
    return pltpu.CompilerParams(vmem_limit_bytes=VMEM_LIMIT)


def cost(flops, bytes_accessed, transcendentals=0):
    return pl.CostEstimate(
        flops=flops, bytes_accessed=bytes_accessed, transcendentals=transcendentals
    )


def pack(heads, reach, table, proj, datt, gains):
    rows = proj.shape[1]
    slot = jax.ShapeDtypeStruct((rows, 4 * HS), BF16)
    count = 2 * reach + 1
    return pl.pallas_call(
        functools.partial(pack_kernel, heads, reach),
        out_shape=[slot] * count + [jax.ShapeDtypeStruct((heads, rows, 4 * HS), BF16)],
        in_specs=[in_smem(), in_vmem(), in_vmem(), in_vmem()],
        out_specs=[in_vmem()] * (count + 1),
        compiler_params=compiler_params(),
        cost_estimate=cost(10**9, 10**7),
    )(table, proj, datt, gains)


def work(reach, tok_rows, table, blocks):
    count = 2 * reach + 1
    max_tiles = -(-(LONG_LEN + 15) // TILE)
    padded = count * tok_rows + GROUP * TILE
    span = max_tiles * TILE
    return pl.pallas_call(
        functools.partial(work_kernel, reach, tok_rows, max_tiles),
        out_shape=[jax.ShapeDtypeStruct((tok_rows, 4 * HS), BF16)] * count,
        in_specs=[in_smem()] + [anywhere()] * count,
        out_specs=[anywhere()] * count,
        scratch_shapes=[
            pltpu.VMEM((padded, 4 * HS), BF16),
            pltpu.VMEM((padded, 4 * HS), BF16),
            pltpu.VMEM((span, 128), BF16),
            pltpu.VMEM((span, 128), BF16),
            pltpu.VMEM((span, 128), BF16),
            pltpu.VMEM((span, 128), BF16),
            pltpu.VMEM((TILE, span), BF16),
            pltpu.VMEM((HS, span), F32),
            pltpu.VMEM((HS, span), F32),
            pltpu.SemaphoreType.DMA((count,)),
            pltpu.SemaphoreType.DMA((count,)),
        ],
        compiler_params=compiler_params(),
        cost_estimate=cost(3 * 10**10, 10**7, 10**7),
    )(table, *blocks)


def local_work(heads, table, local, ids_row, ids_column):
    return pl.pallas_call(
        functools.partial(local_kernel, heads),
        out_shape=jax.ShapeDtypeStruct(local.shape, BF16),
        in_specs=[in_smem(), in_vmem(), in_vmem(), in_vmem()],
        out_specs=in_vmem(),
        compiler_params=compiler_params(),
        cost_estimate=cost(5 * 10**9, 4 * 10**6, 25 * 10**5),
    )(table, local, ids_row, ids_column)


def unpack(heads, reach, table, proj, gains, local, normed, cot, backs):
    rows = proj.shape[1]
    count = 2 * reach + 1
    width = heads * HS
    return pl.pallas_call(
        functools.partial(unpack_kernel, heads, reach),
        out_shape=[
            jax.ShapeDtypeStruct((rows, width), BF16),
            jax.ShapeDtypeStruct((3, rows, width), BF16),
            jax.ShapeDtypeStruct((2, 128), F32),
            jax.ShapeDtypeStruct((4 * normed.shape[1], width), BF16),
        ],
        in_specs=[in_smem()] + [in_vmem()] * 5 + [anywhere()] * count,
        out_specs=[in_vmem()] * 4,
        scratch_shapes=[
            pltpu.VMEM((count, rows, 4 * HS), BF16),
            pltpu.SemaphoreType.DMA((count,)),
        ],
        compiler_params=compiler_params(),
        cost_estimate=cost(10**9, 10**7),
    )(table, proj, gains, local, normed, cot, *backs)


def on_device(
    tokens,
    image_starts,
    ln_gain,
    w_qkv,
    q_gain,
    k_gain,
    w_up,
    up_bias,
    w_attn_out,
    w_down,
    out_bias,
    cotangent,
):
    tok_rows, half = tokens.shape
    local_width = w_qkv.shape[2]
    heads = local_width // HS
    reach = (LONG_LEN + tok_rows - 2) // tok_rows
    n_seq = lax.axis_size("seq")
    place = lax.axis_index("seq")
    side = lax.axis_index("head")
    assert heads == reach + 1 and n_seq >= heads and heads % 2 == 0
    assert n_seq & (n_seq - 1) == 0 and half == local_width

    def from_peer(block):
        return lax.ppermute(block, "head", [(0, 1), (1, 0)])

    def both_halves(block):
        other = from_peer(block)
        first = jnp.where(side == 0, block, other)
        second = jnp.where(side == 0, other, block)
        return jnp.concatenate([first, second], axis=1)

    def add_over_heads(partial):
        low, high = partial[:, :half], partial[:, half:]
        send = jnp.where(side == 0, high, low).astype(BF16)
        keep = jnp.where(side == 0, low, high)
        return keep + from_peer(send).astype(F32)

    def shifted(block, distance):
        if distance == 0:
            return block
        route = [(i, i + distance) for i in range(n_seq) if 0 <= i + distance < n_seq]
        return lax.ppermute(block, "seq", route)

    table = work_table(image_starts, place, n_seq, tok_rows, reach)
    row_index = jnp.arange(tok_rows, dtype=jnp.int32)
    positions = place * tok_rows + row_index
    ids = jnp.sum((image_starts[None, :] <= positions[:, None]).astype(jnp.int32), axis=1)
    is_local = (row_index >= table[0]) & (row_index < table[1])
    ids_column = jnp.where(is_local, ids, -1)[:, None]
    ids_row = jnp.where(is_local, ids, -2)[None, :]
    gains = jnp.tile(jnp.stack([q_gain, k_gain]), (1, 2))

    gathered = both_halves(tokens)
    cot_whole = both_halves(cotangent)
    normed_f, norm_pull = jax.vjp(layer_norm, gathered.astype(F32), ln_gain)
    normed = normed_f.astype(BF16)
    proj = jnp.einsum("td,dkc->ktc", normed, w_qkv, preferred_element_type=F32)
    d_attended = jnp.einsum("td,cd->tc", cot_whole, w_attn_out, preferred_element_type=F32)
    packed = pack(heads, reach, table, proj, d_attended.astype(BF16), gains)
    packed, normed_ff, cot_ff = lax.optimization_barrier((packed, normed, cot_whole))
    slots, local = packed[:-1], packed[-1]

    arrived = [shifted(slots[reach + d], d) for d in range(reach, -reach - 1, -1)]

    up_input = jnp.dot(normed_ff, w_up, preferred_element_type=F32) + up_bias
    hidden_f, gelu_pull = jax.vjp(exact_gelu, up_input)
    hidden = hidden_f.astype(BF16)
    d_hidden = jnp.einsum("td,fd->tf", cot_ff, w_down, preferred_element_type=F32)
    d_upper_f = gelu_pull(d_hidden)[0]
    d_upper = d_upper_f.astype(BF16)
    grad_down = jnp.einsum("tf,td->fd", hidden, cot_ff, preferred_element_type=F32)
    grad_up = jnp.einsum("td,tf->df", normed_ff, d_upper, preferred_element_type=F32)
    grad_out_bias = jnp.sum(cotangent.astype(F32), axis=0)
    grad_up_bias = jnp.sum(d_upper.astype(F32), axis=0)
    early = (grad_down.astype(BF16), grad_up.astype(BF16))
    early, arrived = lax.optimization_barrier((early, arrived))
    early = lax.psum(early, "seq")
    ffn_out = jnp.dot(hidden, w_down, preferred_element_type=F32)
    ffn_back = jnp.einsum("tf,df->td", d_upper, w_up, preferred_element_type=F32)

    local_out = local_work(heads, table, local, ids_row, ids_column)
    worked = work(reach, tok_rows, table, arrived)
    returned = [shifted(worked[b], b - reach) for b in range(2 * reach + 1)][::-1]
    attended, d_proj, gain_sums, late = unpack(
        heads, reach, table, proj, gains, local_out, normed, cot_whole, returned
    )

    partial_out = jnp.dot(attended, w_attn_out, preferred_element_type=F32) + ffn_out
    summed = add_over_heads(partial_out)
    block_out = (summed + tokens.astype(F32) + out_bias).astype(BF16)
    d_normed = ffn_back + jnp.einsum("ktc,dkc->td", d_proj, w_qkv, preferred_element_type=F32)
    d_input, d_ln = norm_pull(d_normed)
    input_sum = add_over_heads(d_input)
    tokens_grad = (input_sum + cotangent.astype(F32)).astype(BF16)

    half_gain = HS // 2
    gain_total = gain_sums[:, :HS] + gain_sums[:, HS:]
    by_side = [
        jnp.concatenate([d_ln[i * half : (i + 1) * half], gain_total[:, i * half_gain : (i + 1) * half_gain].reshape(-1)])
        for i in range(2)
    ]
    own = jnp.where(side == 0, by_side[0], by_side[1])
    norms = own + from_peer(jnp.where(side == 0, by_side[1], by_side[0]))
    small = jnp.concatenate([norms, grad_up_bias, grad_out_bias])
    small_size = small.shape[0]
    small_rows = -(-small_size // (16 * half)) * 16
    small = jnp.pad(small, (0, small_rows * half - small_size)).reshape(small_rows, half)
    late = SeqSum(late, place, n_seq, small)
    for phase in range(late.phases):
        coming = late.send(phase)
        if phase == 0:
            coming, early = lax.optimization_barrier((coming, early))
        late.receive(phase, coming)
    small = late.small
    sums = late.current.astype(F32)
    width = 2 * half
    qkv_rows = 3 * width
    qkv_sum = sums[:qkv_rows].reshape(3, width, local_width).transpose(1, 0, 2)
    out_sum = jnp.concatenate(jnp.split(sums[qkv_rows:], 2, 0), axis=1)
    small = small.reshape(-1)
    at_up = half + HS
    at_out = at_up + up_bias.shape[0]
    return (
        block_out,
        tokens_grad,
        small[:half],
        qkv_sum,
        small[half : half + half_gain],
        small[half + half_gain : at_up],
        early[1].astype(F32),
        small[at_up:at_out],
        out_sum,
        early[0].astype(F32),
        small[at_out : at_out + half],
    )


def solution(mesh):
    in_specs = (
        P("seq", "head"),
        P(),
        P(),
        P(None, None, "head"),
        P(),
        P(),
        P(None, "head"),
        P("head"),
        P("head", None),
        P("head", None),
        P("head"),
        P("seq", "head"),
    )
    out_specs = (
        P("seq", "head"),
        P("seq", "head"),
        P("head"),
        P(None, None, "head"),
        P("head"),
        P("head"),
        P(None, "head"),
        P("head"),
        P("head", None),
        P("head", None),
        P("head"),
    )
    return jax.shard_map(
        on_device, mesh=mesh, in_specs=in_specs, out_specs=out_specs, check_vma=False
    )
```

```python
import functools

import jax
import jax.numpy as jnp
from jax import lax
from jax.experimental import pallas as pl
from jax.experimental.pallas import tpu as pltpu
from jax.sharding import PartitionSpec as P

HS = 64
LONG_LEN = 3136
EPSILON = 1e-06
F32 = jnp.float32
BF16 = jnp.bfloat16
TILE = 256
GROUP = 4
VMEM_LIMIT = 60 * 1024 * 1024


def layer_norm(values, gain_row):
    row_mean = jnp.mean(values, axis=-1, keepdims=True)
    centred = values - row_mean
    spread = jnp.mean(centred * centred, axis=-1, keepdims=True)
    return centred * lax.rsqrt(spread + EPSILON) * gain_row


def exact_gelu(values):
    return jax.nn.gelu(values, approximate=False)


def dot_nn(a, b):
    return lax.dot_general(a, b, (((1,), (0,)), ((), ())), preferred_element_type=F32)


def dot_nt(a, b):
    return lax.dot_general(a, b, (((1,), (1,)), ((), ())), preferred_element_type=F32)


def dot_tn(a, b):
    return lax.dot_general(a, b, (((0,), (0,)), ((), ())), preferred_element_type=F32)


def half_means(block):
    left = (lax.broadcasted_iota(jnp.int32, (256, 128), 0) % 128) // HS
    right = lax.broadcasted_iota(jnp.int32, (256, 128), 1) // HS
    averager = jnp.where(left == right, 1.0 / HS, 0.0).astype(BF16)
    coarse = block.astype(BF16)
    fine = (block - coarse.astype(F32)).astype(BF16)
    return dot_nn(jnp.concatenate([coarse, fine], axis=1), averager)


def normalized_halves(block):
    centred = block - half_means(block)
    inverse = lax.rsqrt(half_means(centred * centred) + EPSILON)
    return centred * inverse, inverse


def work_table(image_starts, place, n_seq, tok_rows, reach):
    window = reach + 1
    total = n_seq * tok_rows
    candidates = jnp.arange(2 * reach, dtype=jnp.int32) + place - reach
    positions = jnp.concatenate(
        [(candidates + 1) * tok_rows - 1, jnp.stack([place * tok_rows, (place + 1) * tok_rows - 1])]
    )
    below = image_starts[None, :] <= positions[:, None]
    starts = jnp.max(jnp.where(below, image_starts[None, :], -1), axis=1)
    ends = jnp.min(jnp.where(below, total, image_starts[None, :]), axis=1)
    first = starts // tok_rows
    last = (ends - 1) // tok_rows
    base = jnp.minimum(first, n_seq - window)
    spans = last > first
    mine = (
        (candidates >= 0)
        & (candidates < n_seq)
        & (first[:-2] == candidates)
        & spans[:-2]
        & (base[:-2] <= place)
        & (base[:-2] >= place - reach)
    )
    lengths = jnp.where(mine, ends[:-2] - starts[:-2], 0)
    rows = jnp.where(mine, starts[:-2] - (place - reach) * tok_rows, 0)
    low_end = jnp.where(spans[-2], jnp.clip(ends[-2] - place * tok_rows, 0, tok_rows), 0)
    low_end = jnp.where(first[-2] < place, low_end, 0)
    high_start = jnp.clip(starts[-1] - place * tok_rows, 0, tok_rows)
    high_start = jnp.where(last[-1] > place, high_start, tok_rows)
    head_part = jnp.stack([low_end, high_start, place - base[-2], place - base[-1]])
    turns = jnp.remainder(-base[-2:], window)
    return jnp.concatenate([head_part, rows, lengths, turns]).astype(jnp.int32)


def pack_kernel(heads, spot, proj, datt, gains, local, *refs):
    slots, sems = refs[:heads], refs[heads]
    rows = proj.shape[1]
    low = lax.broadcasted_iota(jnp.int32, (rows, 128), 1) < HS
    q_gain = gains[0:1, :] * (HS**-0.5)
    k_gain = gains[1:2, :]
    for pair in range(heads // 2):
        lanes = slice(pair * 128, (pair + 1) * 128)
        q = normalized_halves(proj[0, :, lanes])[0] * q_gain
        k = normalized_halves(proj[1, :, lanes])[0] * k_gain
        v = proj[2, :, lanes]
        d = datt[:, lanes].astype(F32)
        q, k, v = (t.astype(BF16).astype(F32) for t in (q, k, v))
        local[2 * pair, :, 0:128] = jnp.where(low, q, pltpu.roll(k, HS, 1)).astype(BF16)
        local[2 * pair, :, 128:256] = jnp.where(low, v, pltpu.roll(d, HS, 1)).astype(BF16)
        local[2 * pair + 1, :, 0:128] = jnp.where(low, pltpu.roll(q, HS, 1), k).astype(BF16)
        local[2 * pair + 1, :, 128:256] = jnp.where(low, pltpu.roll(v, HS, 1), d).astype(BF16)

    def copy_out(turn):
        return pltpu.make_async_copy(
            local.at[lax.rem(spot[0] + turn, heads)], slots[turn], sems.at[turn]
        )

    for turn in range(heads):
        copy_out(turn).start()
    for turn in range(heads):
        copy_out(turn).wait()


def softmax_tail(mixed, d_out):
    lane = lax.broadcasted_iota(jnp.int32, mixed.shape, 1)
    total = mixed[:, HS : HS + 1]
    inverse = 1.0 / jnp.where(total > 0, total, 1.0)
    mixture = mixed * inverse
    delta = jnp.sum(d_out * mixture, axis=1, keepdims=True)
    shift = -delta * inverse
    coarse = shift.astype(BF16).astype(F32)
    scaled = jnp.where(lane == HS, coarse, jnp.where(lane == HS + 1, shift - coarse, d_out * inverse))
    return mixture, scaled.astype(BF16)


def work_kernel(reach, tok_rows, max_tiles, table, *refs):
    count = 2 * reach + 1
    inputs, outputs = refs[:count], refs[count : 2 * count]
    x, y, qb, kb, vb, db, eb, dk, dv, in_sem, out_sem = refs[2 * count :]

    def copy_in(b):
        return pltpu.make_async_copy(inputs[b], x.at[pl.ds(b * tok_rows, tok_rows)], in_sem.at[b])

    def copy_out(b):
        return pltpu.make_async_copy(y.at[pl.ds(b * tok_rows, tok_rows)], outputs[b], out_sem.at[b])

    for b in range(count):
        copy_in(b).start()
    for b in range(count):
        copy_in(b).wait()
    row = lax.broadcasted_iota(jnp.int32, (TILE, 128), 0)
    lane = lax.broadcasted_iota(jnp.int32, (TILE, 128), 1)
    low = lane < HS

    @pl.loop(0, 2 * reach)
    def _(job):
        length = table[4 + 2 * reach + job]
        first = table[4 + job]
        aligned = pl.multiple_of((first // 16) * 16, 16)
        lead = first - aligned
        tiles = (lead + length + TILE - 1) // TILE
        tiles = jnp.where(length > 0, tiles, 0)
        groups = (tiles + GROUP - 1) // GROUP
        grouped = (tiles > 2) & (tiles < max_tiles)
        prepared = jnp.where(grouped, groups * GROUP, tiles)

        def inside(t):
            at = row + t * TILE
            return (at >= lead) & (at < lead + length)

        @pl.loop(0, prepared)
        def _(t):
            at = pl.multiple_of(t * TILE, TILE)
            source = pl.ds(aligned + at, TILE)
            ours = inside(t)
            keep = low & ours
            qk = x[source, 0:128].astype(F32)
            vd = x[source, 128:256].astype(F32)
            ones = jnp.where(lane < HS + 2, 1.0, 0.0)
            qb[pl.ds(at, TILE), :] = jnp.where(keep, qk, 0.0).astype(BF16)
            kb[pl.ds(at, TILE), :] = jnp.where(keep, pltpu.roll(qk, HS, 1), 0.0).astype(BF16)
            vb[pl.ds(at, TILE), :] = jnp.where(ours, jnp.where(low, vd, ones), 0.0).astype(BF16)
            db[pl.ds(at, TILE), :] = jnp.where(keep, pltpu.roll(vd, HS, 1), 0.0).astype(BF16)
            dk[:, pl.ds(at, TILE)] = jnp.zeros((HS, TILE), F32)
            dv[:, pl.ds(at, TILE)] = jnp.zeros((HS, TILE), F32)

        def store(t, lanes, value):
            place = pl.ds(aligned + pl.multiple_of(t * TILE, TILE), TILE)
            old = y[place, lanes].astype(F32)
            y[place, lanes] = jnp.where(inside(t), value, old).astype(BF16)

        def first_pass(q, at):
            e = jnp.exp(dot_nt(q, kb[at, :])).astype(BF16)
            eb[:, at] = e

        def second_pass(q, scaled, at):
            e = eb[:, at]
            dv[:, at] += dot_tn(scaled[:, :HS], e)
            grad = dot_nt(scaled, vb[at, :])
            ds = (e.astype(F32) * grad).astype(BF16)
            eb[:, at] = ds
            dk[:, at] += dot_tn(q[:, :HS], ds)

        @pl.when(tiles == max_tiles)
        def _():
            @pl.loop(0, max_tiles)
            def _(t):
                at = pl.ds(pl.multiple_of(t * TILE, TILE), TILE)
                q = qb[at, :]
                for s in range(max_tiles):
                    first_pass(q, slice(s * TILE, (s + 1) * TILE))
                mixture, scaled = softmax_tail(dot_nn(eb[...], vb[...]), db[at, :].astype(F32))
                for s in range(max_tiles):
                    second_pass(q, scaled, slice(s * TILE, (s + 1) * TILE))
                d_query = dot_nn(eb[...], kb[...])
                store(t, slice(0, 128), jnp.where(low, mixture, pltpu.roll(d_query, HS, 1)))

        @pl.when(grouped)
        def _():
            @pl.loop(0, tiles)
            def _(t):
                at = pl.ds(pl.multiple_of(t * TILE, TILE), TILE)
                q = qb[at, :]

                def mix(g, total):
                    for s in range(GROUP):
                        first_pass(q, pl.ds(pl.multiple_of((g * GROUP + s) * TILE, TILE), TILE))
                    to = pl.ds(pl.multiple_of(g * GROUP * TILE, GROUP * TILE), GROUP * TILE)
                    return total + dot_nn(eb[:, to], vb[to, :])

                mixed = lax.fori_loop(0, groups, mix, jnp.zeros((TILE, 128), F32))
                mixture, scaled = softmax_tail(mixed, db[at, :].astype(F32))

                def back(g, total):
                    for s in range(GROUP):
                        to = pl.ds(pl.multiple_of((g * GROUP + s) * TILE, TILE), TILE)
                        second_pass(q, scaled, to)
                    to = pl.ds(pl.multiple_of(g * GROUP * TILE, GROUP * TILE), GROUP * TILE)
                    return total + dot_nn(eb[:, to], kb[to, :])

                d_query = lax.fori_loop(0, groups, back, jnp.zeros((TILE, 128), F32))
                store(t, slice(0, 128), jnp.where(low, mixture, pltpu.roll(d_query, HS, 1)))

        @pl.when((tiles > 0) & (tiles <= 2))
        def _():
            @pl.loop(0, tiles)
            def _(t):
                at = pl.ds(pl.multiple_of(t * TILE, TILE), TILE)
                q = qb[at, :]

                def mix(s, total):
                    to = pl.ds(pl.multiple_of(s * TILE, TILE), TILE)
                    first_pass(q, to)
                    return total + dot_nn(eb[:, to], vb[to, :])

                mixed = lax.fori_loop(0, tiles, mix, jnp.zeros((TILE, 128), F32))
                mixture, scaled = softmax_tail(mixed, db[at, :].astype(F32))

                def back(s, total):
                    to = pl.ds(pl.multiple_of(s * TILE, TILE), TILE)
                    second_pass(q, scaled, to)
                    return total + dot_nn(eb[:, to], kb[to, :])

                d_query = lax.fori_loop(0, tiles, back, jnp.zeros((TILE, 128), F32))
                store(t, slice(0, 128), jnp.where(low, mixture, pltpu.roll(d_query, HS, 1)))

        @pl.loop(0, tiles)
        def _(t):
            at = pl.ds(pl.multiple_of(t * TILE, TILE), TILE)
            both = jnp.concatenate([dk[:, at], dv[:, at]], axis=0)
            store(t, slice(128, 256), both.T)

    for b in range(count):
        copy_out(b).start()
    for b in range(count):
        copy_out(b).wait()


def local_kernel(heads, table, local, ids_row, ids_column, out):
    rows = local.shape[1]

    @pl.when(table[0] < table[1])
    def _():
        lane = lax.broadcasted_iota(jnp.int32, (rows, 128), 1)
        low = lane < HS
        same = (ids_column[...] == ids_row[...]).astype(F32)
        ones = jnp.where(lane < HS + 2, 1.0, 0.0)

        @pl.loop(0, heads)
        def _(h):
            qk = local[h, :, 0:128].astype(F32)
            vd = local[h, :, 128:256].astype(F32)
            q = jnp.where(low, qk, 0.0).astype(BF16)
            k = jnp.where(low, pltpu.roll(qk, HS, 1), 0.0).astype(BF16)
            v = jnp.where(low, vd, ones).astype(BF16)
            d_out = jnp.where(low, pltpu.roll(vd, HS, 1), 0.0)
            e = (jnp.exp(dot_nt(q, k)) * same).astype(BF16)
            mixture, scaled = softmax_tail(dot_nn(e, v), d_out)
            ds = (e.astype(F32) * dot_nt(scaled, v)).astype(BF16)
            d_query = dot_nn(ds, k)
            d_key = dot_tn(q[:, :HS], ds)
            d_value = dot_tn(scaled[:, :HS], e)
            out[h, :, 0:128] = jnp.where(low, mixture, pltpu.roll(d_query, HS, 1)).astype(BF16)
            out[h, :, 128:256] = jnp.concatenate([d_key, d_value], axis=0).T.astype(BF16)


def unpack_kernel(heads, reach, table, spot, proj, gains, local, normed, cot, *refs):
    count = 2 * reach + 1
    backs = refs[:count]
    attended, d_proj, gain_sums = refs[count : count + 3]
    blocks = refs[count + 3 : count + 7]
    grads, stacked, sems = refs[count + 7 :]
    rows = proj.shape[1]

    def copy_in(b):
        return pltpu.make_async_copy(backs[b], stacked.at[b], sems.at[b])

    for b in range(count):
        copy_in(b).start()
    for b in range(count):
        copy_in(b).wait()
    low = lax.broadcasted_iota(jnp.int32, (rows, 128), 1) < HS
    row = lax.broadcasted_iota(jnp.int32, (rows, 256), 0)
    from_low = row < table[0]
    from_high = row >= table[1]
    q_gain = gains[0:1, :] * (HS**-0.5)
    k_gain = gains[1:2, :]

    def gathered(h):
        lower = stacked[lax.rem(h + table[4 + 4 * reach], heads) - table[2] + reach].astype(F32)
        upper = stacked[lax.rem(h + table[5 + 4 * reach], heads) - table[3] + reach].astype(F32)
        return jnp.where(from_low, lower, jnp.where(from_high, upper, local[h].astype(F32)))

    def back(raw, gradient, gain):
        hat, inverse = normalized_halves(raw)
        scaled = gradient * gain
        shifted = scaled - half_means(scaled) - hat * half_means(scaled * hat)
        return shifted * inverse, jnp.sum(gradient * hat, axis=0, keepdims=True)

    q_sum = jnp.zeros((1, 128), F32)
    k_sum = jnp.zeros((1, 128), F32)
    for pair in range(heads // 2):
        lanes = slice(pair * 128, (pair + 1) * 128)
        even, odd = gathered(2 * pair), gathered(2 * pair + 1)
        mixture = jnp.where(low, even[:, 0:128], pltpu.roll(odd[:, 0:128], HS, 1))
        d_query = jnp.where(low, pltpu.roll(even[:, 0:128], HS, 1), odd[:, 0:128])
        d_key = jnp.where(low, even[:, 128:256], pltpu.roll(odd[:, 128:256], HS, 1))
        d_value = jnp.where(low, pltpu.roll(even[:, 128:256], HS, 1), odd[:, 128:256])
        attended[:, lanes] = mixture.astype(BF16)
        q_raw, q_part = back(proj[0, :, lanes], d_query, q_gain)
        k_raw, k_part = back(proj[1, :, lanes], d_key, k_gain)
        q_sum += q_part
        k_sum += k_part
        d_proj[0, :, lanes] = q_raw.astype(BF16)
        d_proj[1, :, lanes] = k_raw.astype(BF16)
        d_proj[2, :, lanes] = d_value.astype(BF16)
    gain_sums[...] = jnp.concatenate([q_sum * (HS**-0.5), k_sum], axis=0)
    width, columns = normed.shape[1], heads * HS

    for part in range(4):
        if part < 3:
            grads[part] = dot_tn(normed[...], d_proj[part]).astype(BF16)
        else:
            for at in range(0, width, columns):
                grads[part, at : at + columns, :] = dot_tn(
                    attended[...], cot[:, at : at + columns]
                ).astype(BF16)
    for index, block in enumerate(blocks):
        pltpu.make_async_copy(grads.at[index ^ spot[0]], block, sems.at[index]).start()
    for index, block in enumerate(blocks):
        pltpu.make_async_copy(grads.at[index ^ spot[0]], block, sems.at[index]).wait()


class SeqSum:
    def __init__(self, blocks, place, n_seq, small=None):
        width = n_seq.bit_length() - 1
        self.n_seq = n_seq
        stages = [(bit, 1 << min(2, width - bit)) for bit in range(0, width, 2)]
        self.order = stages + stages[::-1]
        self.phases = len(self.order)
        self.codes = {bit: (place >> bit) & (radix - 1) for bit, radix in stages}
        self.blocks, self.current, self.small = blocks, None, small

    def describe(self, phase):
        bit, radix = self.order[phase]
        adding = phase < self.phases // 2
        joins = self.small is not None and adding == (bit > 0)
        return bit, radix, adding, joins, self.codes[bit]

    def block(self, phase, mask):
        bit, radix, _, _, code = self.describe(phase)
        if phase == 0:
            return self.blocks[mask]
        rows, lanes = self.current.shape
        split = self.current.reshape(radix, rows // radix, lanes)
        return lax.dynamic_index_in_dim(split, code ^ mask, 0, keepdims=False)

    def send(self, phase):
        bit, radix, adding, joins, code = self.describe(phase)
        tail = self.small.astype(BF16) if joins else None
        arrived = []
        for mask in reversed(range(1, radix)):
            block = self.current
            if adding:
                block = self.block(phase, mask)
            if joins:
                block = jnp.concatenate([block, tail], axis=0)
            route = [(i, i ^ (mask << bit)) for i in range(self.n_seq)]
            arrived.append(lax.ppermute(block, "seq", route))
        return arrived

    def receive(self, phase, arrived):
        bit, radix, adding, joins, code = self.describe(phase)
        own = self.block(phase, 0) if adding else self.current
        height, lanes = own.shape
        if adding:
            total = own.astype(F32)
            for block in arrived:
                total = total + block[:height].astype(F32)
            self.current = total.astype(BF16)
        else:
            whole = jnp.zeros((radix, height, lanes), BF16)
            whole = lax.dynamic_update_index_in_dim(whole, self.current, code, 0)
            for mask, block in zip(reversed(range(1, radix)), arrived):
                whole = lax.dynamic_update_index_in_dim(whole, block[:height], code ^ mask, 0)
            self.current = whole.reshape(radix * height, lanes)
        if joins:
            small = self.small.astype(BF16).astype(F32)
            for block in arrived:
                small = small + block[height:].astype(F32)
            self.small = small


def in_vmem():
    return pl.BlockSpec(memory_space=pltpu.VMEM)


def in_smem():
    return pl.BlockSpec(memory_space=pltpu.SMEM)


def anywhere():
    return pl.BlockSpec(memory_space=pl.ANY)


def compiler_params():
    return pltpu.CompilerParams(vmem_limit_bytes=VMEM_LIMIT)


def cost(flops, bytes_accessed, transcendentals=0):
    return pl.CostEstimate(
        flops=flops, bytes_accessed=bytes_accessed, transcendentals=transcendentals
    )


def pack(heads, spot, proj, datt, gains):
    rows = proj.shape[1]
    slot = jax.ShapeDtypeStruct((rows, 4 * HS), BF16)
    return pl.pallas_call(
        functools.partial(pack_kernel, heads),
        out_shape=[jax.ShapeDtypeStruct((heads, rows, 4 * HS), BF16)] + [slot] * heads,
        in_specs=[in_smem(), in_vmem(), in_vmem(), in_vmem()],
        out_specs=[in_vmem()] + [anywhere()] * heads,
        scratch_shapes=[pltpu.SemaphoreType.DMA((heads,))],
        compiler_params=compiler_params(),
        cost_estimate=cost(10**9, 10**7),
    )(spot, proj, datt, gains)


def work(reach, tok_rows, table, blocks):
    count = 2 * reach + 1
    max_tiles = -(-(LONG_LEN + 15) // TILE)
    padded = count * tok_rows + GROUP * TILE
    span = max_tiles * TILE
    return pl.pallas_call(
        functools.partial(work_kernel, reach, tok_rows, max_tiles),
        out_shape=[jax.ShapeDtypeStruct((tok_rows, 4 * HS), BF16)] * count,
        in_specs=[in_smem()] + [anywhere()] * count,
        out_specs=[anywhere()] * count,
        scratch_shapes=[
            pltpu.VMEM((padded, 4 * HS), BF16),
            pltpu.VMEM((padded, 4 * HS), BF16),
            pltpu.VMEM((span, 128), BF16),
            pltpu.VMEM((span, 128), BF16),
            pltpu.VMEM((span, 128), BF16),
            pltpu.VMEM((span, 128), BF16),
            pltpu.VMEM((TILE, span), BF16),
            pltpu.VMEM((HS, span), F32),
            pltpu.VMEM((HS, span), F32),
            pltpu.SemaphoreType.DMA((count,)),
            pltpu.SemaphoreType.DMA((count,)),
        ],
        compiler_params=compiler_params(),
        cost_estimate=cost(3 * 10**10, 10**7, 10**7),
    )(table, *blocks)


def local_work(heads, table, local, ids_row, ids_column):
    return pl.pallas_call(
        functools.partial(local_kernel, heads),
        out_shape=jax.ShapeDtypeStruct(local.shape, BF16),
        in_specs=[in_smem(), in_vmem(), in_vmem(), in_vmem()],
        out_specs=in_vmem(),
        compiler_params=compiler_params(),
        cost_estimate=cost(5 * 10**9, 4 * 10**6, 25 * 10**5),
    )(table, local, ids_row, ids_column)


def unpack(heads, reach, table, spot, proj, gains, local, normed, cot, backs):
    rows = proj.shape[1]
    count = 2 * reach + 1
    width = heads * HS
    return pl.pallas_call(
        functools.partial(unpack_kernel, heads, reach),
        out_shape=[
            jax.ShapeDtypeStruct((rows, width), BF16),
            jax.ShapeDtypeStruct((3, rows, width), BF16),
            jax.ShapeDtypeStruct((2, 128), F32),
        ]
        + [jax.ShapeDtypeStruct((normed.shape[1], width), BF16)] * 4,
        in_specs=[in_smem()] * 2 + [in_vmem()] * 5 + [anywhere()] * count,
        out_specs=[in_vmem()] * 3 + [anywhere()] * 4,
        scratch_shapes=[
            pltpu.VMEM((4, normed.shape[1], width), BF16),
            pltpu.VMEM((count, rows, 4 * HS), BF16),
            pltpu.SemaphoreType.DMA((count,)),
        ],
        compiler_params=compiler_params(),
        cost_estimate=cost(10**9, 10**7),
    )(table, spot, proj, gains, local, normed, cot, *backs)


def on_device(
    tokens,
    image_starts,
    ln_gain,
    w_qkv,
    q_gain,
    k_gain,
    w_up,
    up_bias,
    w_attn_out,
    w_down,
    out_bias,
    cotangent,
):
    tok_rows, half = tokens.shape
    local_width = w_qkv.shape[2]
    heads = local_width // HS
    reach = (LONG_LEN + tok_rows - 2) // tok_rows
    n_seq = lax.axis_size("seq")
    place = lax.axis_index("seq")
    side = lax.axis_index("head")
    assert heads == reach + 1 and n_seq >= heads and heads % 2 == 0
    assert n_seq & (n_seq - 1) == 0 and half == local_width

    def from_peer(block):
        return lax.ppermute(block, "head", [(0, 1), (1, 0)])

    def both_halves(block):
        other = from_peer(block)
        first = jnp.where(side == 0, block, other)
        second = jnp.where(side == 0, other, block)
        return jnp.concatenate([first, second], axis=1)

    def add_over_heads(partial):
        low, high = partial[:, :half], partial[:, half:]
        send = jnp.where(side == 0, high, low).astype(BF16)
        keep = jnp.where(side == 0, low, high)
        return keep + from_peer(send).astype(F32)

    def shifted(block, distance):
        if distance == 0:
            return block
        route = [(i, i + distance) for i in range(n_seq) if 0 <= i + distance < n_seq]
        return lax.ppermute(block, "seq", route)

    gains = jnp.tile(jnp.stack([q_gain, k_gain]), (1, 2))

    gathered = both_halves(tokens)
    cot_whole = both_halves(cotangent)
    normed_f, norm_pull = jax.vjp(layer_norm, gathered.astype(F32), ln_gain)
    normed = normed_f.astype(BF16)
    proj = jnp.einsum("td,dkc->ktc", normed, w_qkv, preferred_element_type=F32)
    d_attended = jnp.einsum("td,cd->tc", cot_whole, w_attn_out, preferred_element_type=F32)
    spot = jnp.reshape(place, (1,)).astype(jnp.int32)
    packed = pack(heads, spot, proj, d_attended.astype(BF16), gains)
    packed, image_starts = lax.optimization_barrier((packed, image_starts))
    local, slots = packed[0], packed[1:]

    arrived = [shifted(slots[d % heads], d) for d in range(reach, -reach - 1, -1)]
    table = work_table(image_starts, place, n_seq, tok_rows, reach)
    row_index = jnp.arange(tok_rows, dtype=jnp.int32)
    positions = place * tok_rows + row_index
    ids = jnp.sum((image_starts[None, :] <= positions[:, None]).astype(jnp.int32), axis=1)
    is_local = (row_index >= table[0]) & (row_index < table[1])
    ids_column = jnp.where(is_local, ids, -1)[:, None]
    ids_row = jnp.where(is_local, ids, -2)[None, :]

    arrived[0], normed_ff, cot_ff = lax.optimization_barrier((arrived[0], normed, cot_whole))
    up_input = jnp.dot(normed_ff, w_up, preferred_element_type=F32) + up_bias
    hidden_f, gelu_pull = jax.vjp(exact_gelu, up_input)
    hidden = hidden_f.astype(BF16)
    d_hidden = jnp.einsum("td,fd->tf", cot_ff, w_down, preferred_element_type=F32)
    d_upper_f = gelu_pull(d_hidden)[0]
    d_upper = d_upper_f.astype(BF16)
    grad_down = jnp.einsum("tf,td->fd", hidden, cot_ff, preferred_element_type=F32)
    grad_up = jnp.einsum("td,tf->df", normed_ff, d_upper, preferred_element_type=F32)
    grad_out_bias = jnp.sum(cotangent.astype(F32), axis=0)
    grad_up_bias = jnp.sum(d_upper.astype(F32), axis=0)
    early = (grad_down.astype(BF16), grad_up.astype(BF16))
    early = lax.psum(early, "seq")
    ffn_out = jnp.dot(hidden, w_down, preferred_element_type=F32)
    ffn_back = jnp.einsum("tf,df->td", d_upper, w_up, preferred_element_type=F32)

    worked = list(work(reach, tok_rows, table, arrived))
    worked[0], local = lax.optimization_barrier((worked[0], local))
    local_out = local_work(heads, table, local, ids_row, ids_column)
    returned = [shifted(worked[b], b - reach) for b in range(2 * reach + 1)][::-1]
    corner = jnp.bitwise_and(spot, 3)
    attended, d_proj, gain_sums, *late = unpack(
        heads, reach, table, corner, proj, gains, local_out, normed, cot_whole, returned
    )

    partial_out = jnp.dot(attended, w_attn_out, preferred_element_type=F32) + ffn_out
    summed = add_over_heads(partial_out)
    block_out = (summed + tokens.astype(F32) + out_bias).astype(BF16)
    d_normed = ffn_back + jnp.einsum("ktc,dkc->td", d_proj, w_qkv, preferred_element_type=F32)
    d_input, d_ln = norm_pull(d_normed)
    input_sum = add_over_heads(d_input)
    tokens_grad = (input_sum + cotangent.astype(F32)).astype(BF16)

    half_gain = HS // 2
    gain_total = gain_sums[:, :HS] + gain_sums[:, HS:]
    by_side = [
        jnp.concatenate([d_ln[i * half : (i + 1) * half], gain_total[:, i * half_gain : (i + 1) * half_gain].reshape(-1)])
        for i in range(2)
    ]
    own = jnp.where(side == 0, by_side[0], by_side[1])
    norms = own + from_peer(jnp.where(side == 0, by_side[1], by_side[0]))
    small = jnp.concatenate([norms, grad_up_bias, grad_out_bias])
    small_size = small.shape[0]
    small_rows = -(-small_size // (16 * half)) * 16
    small = jnp.pad(small, (0, small_rows * half - small_size)).reshape(small_rows, half)
    late = SeqSum(late, place, n_seq, small)
    for phase in range(late.phases):
        coming = late.send(phase)
        if phase == 0:
            coming, early = lax.optimization_barrier((coming, early))
        late.receive(phase, coming)
    small = late.small
    sums = late.current.astype(F32)
    width = 2 * half
    qkv_rows = 3 * width
    qkv_sum = sums[:qkv_rows].reshape(3, width, local_width).transpose(1, 0, 2)
    out_sum = jnp.concatenate(jnp.split(sums[qkv_rows:], 2, 0), axis=1)
    small = small.reshape(-1)
    at_up = half + HS
    at_out = at_up + up_bias.shape[0]
    return (
        block_out,
        tokens_grad,
        small[:half],
        qkv_sum,
        small[half : half + half_gain],
        small[half + half_gain : at_up],
        early[1].astype(F32),
        small[at_up:at_out],
        out_sum,
        early[0].astype(F32),
        small[at_out : at_out + half],
    )


def solution(mesh):
    in_specs = (
        P("seq", "head"),
        P(),
        P(),
        P(None, None, "head"),
        P(),
        P(),
        P(None, "head"),
        P("head"),
        P("head", None),
        P("head", None),
        P("head"),
        P("seq", "head"),
    )
    out_specs = (
        P("seq", "head"),
        P("seq", "head"),
        P("head"),
        P(None, None, "head"),
        P("head"),
        P("head"),
        P(None, "head"),
        P("head"),
        P("head", None),
        P("head", None),
        P("head"),
    )
    return jax.shard_map(
        on_device, mesh=mesh, in_specs=in_specs, out_specs=out_specs, check_vma=False
    )
```

```python
import functools

import jax
import jax.numpy as jnp
from jax import lax
from jax.experimental import pallas as pl
from jax.experimental.pallas import tpu as pltpu
from jax.sharding import PartitionSpec as P

HS = 64
LONG_LEN = 3136
EPSILON = 1e-06
F32 = jnp.float32
BF16 = jnp.bfloat16
TILE = 256
GROUP = 4
VMEM_LIMIT = 60 * 1024 * 1024


def layer_norm(values, gain_row):
    row_mean = jnp.mean(values, axis=-1, keepdims=True)
    centred = values - row_mean
    spread = jnp.mean(centred * centred, axis=-1, keepdims=True)
    return centred * lax.rsqrt(spread + EPSILON) * gain_row


def exact_gelu(values):
    return jax.nn.gelu(values, approximate=False)


def dot_nn(a, b):
    return lax.dot_general(a, b, (((1,), (0,)), ((), ())), preferred_element_type=F32)


def dot_nt(a, b):
    return lax.dot_general(a, b, (((1,), (1,)), ((), ())), preferred_element_type=F32)


def dot_tn(a, b):
    return lax.dot_general(a, b, (((0,), (0,)), ((), ())), preferred_element_type=F32)


def half_means(block):
    left = (lax.broadcasted_iota(jnp.int32, (256, 128), 0) % 128) // HS
    right = lax.broadcasted_iota(jnp.int32, (256, 128), 1) // HS
    averager = jnp.where(left == right, 1.0 / HS, 0.0).astype(BF16)
    coarse = block.astype(BF16)
    fine = (block - coarse.astype(F32)).astype(BF16)
    return dot_nn(jnp.concatenate([coarse, fine], axis=1), averager)


def normalized_halves(block):
    centred = block - half_means(block)
    inverse = lax.rsqrt(half_means(centred * centred) + EPSILON)
    return centred * inverse, inverse


def work_table(image_starts, place, n_seq, tok_rows, reach):
    window = reach + 1
    total = n_seq * tok_rows
    candidates = jnp.arange(2 * reach, dtype=jnp.int32) + place - reach
    positions = jnp.concatenate(
        [(candidates + 1) * tok_rows - 1, jnp.stack([place * tok_rows, (place + 1) * tok_rows - 1])]
    )
    below = image_starts[None, :] <= positions[:, None]
    starts = jnp.max(jnp.where(below, image_starts[None, :], -1), axis=1)
    ends = jnp.min(jnp.where(below, total, image_starts[None, :]), axis=1)
    first = starts // tok_rows
    last = (ends - 1) // tok_rows
    base = jnp.minimum(first, n_seq - window)
    spans = last > first
    mine = (
        (candidates >= 0)
        & (candidates < n_seq)
        & (first[:-2] == candidates)
        & spans[:-2]
        & (base[:-2] <= place)
        & (base[:-2] >= place - reach)
    )
    lengths = jnp.where(mine, ends[:-2] - starts[:-2], 0)
    rows = jnp.where(mine, starts[:-2] - (place - reach) * tok_rows, 0)
    low_end = jnp.where(spans[-2], jnp.clip(ends[-2] - place * tok_rows, 0, tok_rows), 0)
    low_end = jnp.where(first[-2] < place, low_end, 0)
    high_start = jnp.clip(starts[-1] - place * tok_rows, 0, tok_rows)
    high_start = jnp.where(last[-1] > place, high_start, tok_rows)
    head_part = jnp.stack([low_end, high_start, place - base[-2], place - base[-1]])
    turns = jnp.remainder(-base[-2:], window)
    return jnp.concatenate([head_part, rows, lengths, turns]).astype(jnp.int32)


def pack_kernel(heads, spot, proj, datt, gains, local, *refs):
    slots, sems = refs[:heads], refs[heads]
    rows = proj.shape[1]
    low = lax.broadcasted_iota(jnp.int32, (rows, 128), 1) < HS
    q_gain = gains[0:1, :] * (HS**-0.5)
    k_gain = gains[1:2, :]
    for pair in range(heads // 2):
        lanes = slice(pair * 128, (pair + 1) * 128)
        q = normalized_halves(proj[0, :, lanes])[0] * q_gain
        k = normalized_halves(proj[1, :, lanes])[0] * k_gain
        v = proj[2, :, lanes]
        d = datt[:, lanes].astype(F32)
        q, k, v = (t.astype(BF16).astype(F32) for t in (q, k, v))
        local[2 * pair, :, 0:128] = jnp.where(low, q, pltpu.roll(k, HS, 1)).astype(BF16)
        local[2 * pair, :, 128:256] = jnp.where(low, v, pltpu.roll(d, HS, 1)).astype(BF16)
        local[2 * pair + 1, :, 0:128] = jnp.where(low, pltpu.roll(q, HS, 1), k).astype(BF16)
        local[2 * pair + 1, :, 128:256] = jnp.where(low, pltpu.roll(v, HS, 1), d).astype(BF16)

    def copy_out(turn):
        return pltpu.make_async_copy(
            local.at[lax.rem(spot[0] + turn, heads)], slots[turn], sems.at[turn]
        )

    for turn in range(heads):
        copy_out(turn).start()
    for turn in range(heads):
        copy_out(turn).wait()


def softmax_tail(mixed, d_out):
    lane = lax.broadcasted_iota(jnp.int32, mixed.shape, 1)
    total = mixed[:, HS : HS + 1]
    inverse = 1.0 / jnp.where(total > 0, total, 1.0)
    mixture = mixed * inverse
    delta = jnp.sum(d_out * mixture, axis=1, keepdims=True)
    shift = -delta * inverse
    coarse = shift.astype(BF16).astype(F32)
    scaled = jnp.where(lane == HS, coarse, jnp.where(lane == HS + 1, shift - coarse, d_out * inverse))
    return mixture, scaled.astype(BF16)


def work_kernel(reach, tok_rows, max_tiles, table, *refs):
    count = 2 * reach + 1
    inputs, outputs = refs[:count], refs[count : 2 * count]
    x, y, qb, kb, vb, db, eb, dk, dv, in_sem, out_sem = refs[2 * count :]

    def copy_in(b):
        return pltpu.make_async_copy(inputs[b], x.at[pl.ds(b * tok_rows, tok_rows)], in_sem.at[b])

    def copy_out(b):
        return pltpu.make_async_copy(y.at[pl.ds(b * tok_rows, tok_rows)], outputs[b], out_sem.at[b])

    for b in range(count):
        copy_in(b).start()
    for b in range(count):
        copy_in(b).wait()
    row = lax.broadcasted_iota(jnp.int32, (TILE, 128), 0)
    lane = lax.broadcasted_iota(jnp.int32, (TILE, 128), 1)
    low = lane < HS

    @pl.loop(0, 2 * reach)
    def _(job):
        length = table[4 + 2 * reach + job]
        first = table[4 + job]
        aligned = pl.multiple_of((first // 16) * 16, 16)
        lead = first - aligned
        tiles = (lead + length + TILE - 1) // TILE
        tiles = jnp.where(length > 0, tiles, 0)
        groups = (tiles + GROUP - 1) // GROUP
        grouped = (tiles > 2) & (tiles < max_tiles)
        prepared = jnp.where(grouped, groups * GROUP, tiles)

        def inside(t):
            at = row + t * TILE
            return (at >= lead) & (at < lead + length)

        @pl.loop(0, prepared)
        def _(t):
            at = pl.multiple_of(t * TILE, TILE)
            source = pl.ds(aligned + at, TILE)
            ours = inside(t)
            keep = low & ours
            qk = x[source, 0:128].astype(F32)
            vd = x[source, 128:256].astype(F32)
            ones = jnp.where(lane < HS + 2, 1.0, 0.0)
            qb[pl.ds(at, TILE), :] = jnp.where(keep, qk, 0.0).astype(BF16)
            kb[pl.ds(at, TILE), :] = jnp.where(keep, pltpu.roll(qk, HS, 1), 0.0).astype(BF16)
            vb[pl.ds(at, TILE), :] = jnp.where(ours, jnp.where(low, vd, ones), 0.0).astype(BF16)
            db[pl.ds(at, TILE), :] = jnp.where(keep, pltpu.roll(vd, HS, 1), 0.0).astype(BF16)
            dk[:, pl.ds(at, TILE)] = jnp.zeros((HS, TILE), F32)
            dv[:, pl.ds(at, TILE)] = jnp.zeros((HS, TILE), F32)

        def store(t, lanes, value):
            place = pl.ds(aligned + pl.multiple_of(t * TILE, TILE), TILE)
            old = y[place, lanes].astype(F32)
            y[place, lanes] = jnp.where(inside(t), value, old).astype(BF16)

        def first_pass(q, at):
            e = jnp.exp(dot_nt(q, kb[at, :])).astype(BF16)
            eb[:, at] = e

        def second_pass(q, scaled, at):
            e = eb[:, at]
            dv[:, at] += dot_tn(scaled[:, :HS], e)
            grad = dot_nt(scaled, vb[at, :])
            ds = (e.astype(F32) * grad).astype(BF16)
            eb[:, at] = ds
            dk[:, at] += dot_tn(q[:, :HS], ds)

        @pl.when(tiles == max_tiles)
        def _():
            @pl.loop(0, max_tiles)
            def _(t):
                at = pl.ds(pl.multiple_of(t * TILE, TILE), TILE)
                q = qb[at, :]
                for s in range(max_tiles):
                    first_pass(q, slice(s * TILE, (s + 1) * TILE))
                mixture, scaled = softmax_tail(dot_nn(eb[...], vb[...]), db[at, :].astype(F32))
                for s in range(max_tiles):
                    second_pass(q, scaled, slice(s * TILE, (s + 1) * TILE))
                d_query = dot_nn(eb[...], kb[...])
                store(t, slice(0, 128), jnp.where(low, mixture, pltpu.roll(d_query, HS, 1)))

        @pl.when(grouped)
        def _():
            @pl.loop(0, tiles)
            def _(t):
                at = pl.ds(pl.multiple_of(t * TILE, TILE), TILE)
                q = qb[at, :]

                def mix(g, total):
                    for s in range(GROUP):
                        first_pass(q, pl.ds(pl.multiple_of((g * GROUP + s) * TILE, TILE), TILE))
                    to = pl.ds(pl.multiple_of(g * GROUP * TILE, GROUP * TILE), GROUP * TILE)
                    return total + dot_nn(eb[:, to], vb[to, :])

                mixed = lax.fori_loop(0, groups, mix, jnp.zeros((TILE, 128), F32))
                mixture, scaled = softmax_tail(mixed, db[at, :].astype(F32))

                def back(g, total):
                    for s in range(GROUP):
                        to = pl.ds(pl.multiple_of((g * GROUP + s) * TILE, TILE), TILE)
                        second_pass(q, scaled, to)
                    to = pl.ds(pl.multiple_of(g * GROUP * TILE, GROUP * TILE), GROUP * TILE)
                    return total + dot_nn(eb[:, to], kb[to, :])

                d_query = lax.fori_loop(0, groups, back, jnp.zeros((TILE, 128), F32))
                store(t, slice(0, 128), jnp.where(low, mixture, pltpu.roll(d_query, HS, 1)))

        @pl.when((tiles > 0) & (tiles <= 2))
        def _():
            @pl.loop(0, tiles)
            def _(t):
                at = pl.ds(pl.multiple_of(t * TILE, TILE), TILE)
                q = qb[at, :]

                def mix(s, total):
                    to = pl.ds(pl.multiple_of(s * TILE, TILE), TILE)
                    first_pass(q, to)
                    return total + dot_nn(eb[:, to], vb[to, :])

                mixed = lax.fori_loop(0, tiles, mix, jnp.zeros((TILE, 128), F32))
                mixture, scaled = softmax_tail(mixed, db[at, :].astype(F32))

                def back(s, total):
                    to = pl.ds(pl.multiple_of(s * TILE, TILE), TILE)
                    second_pass(q, scaled, to)
                    return total + dot_nn(eb[:, to], kb[to, :])

                d_query = lax.fori_loop(0, tiles, back, jnp.zeros((TILE, 128), F32))
                store(t, slice(0, 128), jnp.where(low, mixture, pltpu.roll(d_query, HS, 1)))

        @pl.loop(0, tiles)
        def _(t):
            at = pl.ds(pl.multiple_of(t * TILE, TILE), TILE)
            both = jnp.concatenate([dk[:, at], dv[:, at]], axis=0)
            store(t, slice(128, 256), both.T)

    for b in range(count):
        copy_out(b).start()
    for b in range(count):
        copy_out(b).wait()


def local_kernel(heads, table, local, ids_row, ids_column, out):
    rows = local.shape[1]

    @pl.when(table[0] < table[1])
    def _():
        lane = lax.broadcasted_iota(jnp.int32, (rows, 128), 1)
        low = lane < HS
        same = (ids_column[...] == ids_row[...]).astype(F32)
        ones = jnp.where(lane < HS + 2, 1.0, 0.0)

        @pl.loop(0, heads)
        def _(h):
            qk = local[h, :, 0:128].astype(F32)
            vd = local[h, :, 128:256].astype(F32)
            q = jnp.where(low, qk, 0.0).astype(BF16)
            k = jnp.where(low, pltpu.roll(qk, HS, 1), 0.0).astype(BF16)
            v = jnp.where(low, vd, ones).astype(BF16)
            d_out = jnp.where(low, pltpu.roll(vd, HS, 1), 0.0)
            e = (jnp.exp(dot_nt(q, k)) * same).astype(BF16)
            mixture, scaled = softmax_tail(dot_nn(e, v), d_out)
            ds = (e.astype(F32) * dot_nt(scaled, v)).astype(BF16)
            d_query = dot_nn(ds, k)
            d_key = dot_tn(q[:, :HS], ds)
            d_value = dot_tn(scaled[:, :HS], e)
            out[h, :, 0:128] = jnp.where(low, mixture, pltpu.roll(d_query, HS, 1)).astype(BF16)
            out[h, :, 128:256] = jnp.concatenate([d_key, d_value], axis=0).T.astype(BF16)


def unpack_kernel(heads, reach, table, spot, proj, gains, local, normed, cot, *refs):
    count = 2 * reach + 1
    backs = refs[:count]
    attended, d_proj, gain_sums = refs[count : count + 3]
    blocks = refs[count + 3 : count + 7]
    grads, stacked, sems = refs[count + 7 :]
    rows = proj.shape[1]

    def copy_in(b):
        return pltpu.make_async_copy(backs[b], stacked.at[b], sems.at[b])

    for b in range(count):
        copy_in(b).start()
    for b in range(count):
        copy_in(b).wait()
    low = lax.broadcasted_iota(jnp.int32, (rows, 128), 1) < HS
    row = lax.broadcasted_iota(jnp.int32, (rows, 256), 0)
    from_low = row < table[0]
    from_high = row >= table[1]
    q_gain = gains[0:1, :] * (HS**-0.5)
    k_gain = gains[1:2, :]

    def gathered(h):
        lower = stacked[lax.rem(h + table[4 + 4 * reach], heads) - table[2] + reach].astype(F32)
        upper = stacked[lax.rem(h + table[5 + 4 * reach], heads) - table[3] + reach].astype(F32)
        return jnp.where(from_low, lower, jnp.where(from_high, upper, local[h].astype(F32)))

    def back(raw, gradient, gain):
        hat, inverse = normalized_halves(raw)
        scaled = gradient * gain
        shifted = scaled - half_means(scaled) - hat * half_means(scaled * hat)
        return shifted * inverse, jnp.sum(gradient * hat, axis=0, keepdims=True)

    q_sum = jnp.zeros((1, 128), F32)
    k_sum = jnp.zeros((1, 128), F32)
    for pair in range(heads // 2):
        lanes = slice(pair * 128, (pair + 1) * 128)
        even, odd = gathered(2 * pair), gathered(2 * pair + 1)
        mixture = jnp.where(low, even[:, 0:128], pltpu.roll(odd[:, 0:128], HS, 1))
        d_query = jnp.where(low, pltpu.roll(even[:, 0:128], HS, 1), odd[:, 0:128])
        d_key = jnp.where(low, even[:, 128:256], pltpu.roll(odd[:, 128:256], HS, 1))
        d_value = jnp.where(low, pltpu.roll(even[:, 128:256], HS, 1), odd[:, 128:256])
        attended[:, lanes] = mixture.astype(BF16)
        q_raw, q_part = back(proj[0, :, lanes], d_query, q_gain)
        k_raw, k_part = back(proj[1, :, lanes], d_key, k_gain)
        q_sum += q_part
        k_sum += k_part
        d_proj[0, :, lanes] = q_raw.astype(BF16)
        d_proj[1, :, lanes] = k_raw.astype(BF16)
        d_proj[2, :, lanes] = d_value.astype(BF16)
    gain_sums[...] = jnp.concatenate([q_sum * (HS**-0.5), k_sum], axis=0)
    width, columns = normed.shape[1], heads * HS

    for part in range(4):
        if part < 3:
            grads[part] = dot_tn(normed[...], d_proj[part]).astype(BF16)
        else:
            for at in range(0, width, columns):
                grads[part, at : at + columns, :] = dot_tn(
                    attended[...], cot[:, at : at + columns]
                ).astype(BF16)
    for index, block in enumerate(blocks):
        pltpu.make_async_copy(grads.at[index ^ spot[0]], block, sems.at[index]).start()
    for index, block in enumerate(blocks):
        pltpu.make_async_copy(grads.at[index ^ spot[0]], block, sems.at[index]).wait()


class SeqSum:
    def __init__(self, blocks, place, n_seq, small=None):
        width = n_seq.bit_length() - 1
        self.n_seq = n_seq
        stages = [(bit, 1 << min(2, width - bit)) for bit in range(0, width, 2)]
        self.order = stages + stages[::-1]
        self.phases = len(self.order)
        self.codes = {bit: (place >> bit) & (radix - 1) for bit, radix in stages}
        self.blocks, self.current, self.small = blocks, None, small

    def describe(self, phase):
        bit, radix = self.order[phase]
        adding = phase < self.phases // 2
        joins = self.small is not None and adding == (bit > 0)
        return bit, radix, adding, joins, self.codes[bit]

    def block(self, phase, mask):
        bit, radix, _, _, code = self.describe(phase)
        if phase == 0:
            return self.blocks[mask]
        rows, lanes = self.current.shape
        split = self.current.reshape(radix, rows // radix, lanes)
        return lax.dynamic_index_in_dim(split, code ^ mask, 0, keepdims=False)

    def send(self, phase):
        bit, radix, adding, joins, code = self.describe(phase)
        tail = self.small.astype(BF16) if joins else None
        arrived = []
        for mask in reversed(range(1, radix)):
            block = self.current
            if adding:
                block = self.block(phase, mask)
            if joins:
                block = jnp.concatenate([block, tail], axis=0)
            route = [(i, i ^ (mask << bit)) for i in range(self.n_seq)]
            arrived.append(lax.ppermute(block, "seq", route))
        return arrived

    def receive(self, phase, arrived):
        bit, radix, adding, joins, code = self.describe(phase)
        own = self.block(phase, 0) if adding else self.current
        height, lanes = own.shape
        if adding:
            total = own.astype(F32)
            for block in arrived:
                total = total + block[:height].astype(F32)
            self.current = total.astype(BF16)
        else:
            whole = jnp.zeros((radix, height, lanes), BF16)
            whole = lax.dynamic_update_index_in_dim(whole, self.current, code, 0)
            for mask, block in zip(reversed(range(1, radix)), arrived):
                whole = lax.dynamic_update_index_in_dim(whole, block[:height], code ^ mask, 0)
            self.current = whole.reshape(radix * height, lanes)
        if joins:
            small = self.small.astype(BF16).astype(F32)
            for block in arrived:
                small = small + block[height:].astype(F32)
            self.small = small


def in_vmem():
    return pl.BlockSpec(memory_space=pltpu.VMEM)


def in_smem():
    return pl.BlockSpec(memory_space=pltpu.SMEM)


def anywhere():
    return pl.BlockSpec(memory_space=pl.ANY)


def compiler_params():
    return pltpu.CompilerParams(vmem_limit_bytes=VMEM_LIMIT)


def cost(flops, bytes_accessed, transcendentals=0):
    return pl.CostEstimate(
        flops=flops, bytes_accessed=bytes_accessed, transcendentals=transcendentals
    )


def pack(heads, spot, proj, datt, gains):
    rows = proj.shape[1]
    slot = jax.ShapeDtypeStruct((rows, 4 * HS), BF16)
    return pl.pallas_call(
        functools.partial(pack_kernel, heads),
        out_shape=[jax.ShapeDtypeStruct((heads, rows, 4 * HS), BF16)] + [slot] * heads,
        in_specs=[in_smem(), in_vmem(), in_vmem(), in_vmem()],
        out_specs=[in_vmem()] + [anywhere()] * heads,
        scratch_shapes=[pltpu.SemaphoreType.DMA((heads,))],
        compiler_params=compiler_params(),
        cost_estimate=cost(10**9, 10**7),
    )(spot, proj, datt, gains)


def work(reach, tok_rows, table, blocks):
    count = 2 * reach + 1
    max_tiles = -(-(LONG_LEN + 15) // TILE)
    padded = count * tok_rows + GROUP * TILE
    span = max_tiles * TILE
    return pl.pallas_call(
        functools.partial(work_kernel, reach, tok_rows, max_tiles),
        out_shape=[jax.ShapeDtypeStruct((tok_rows, 4 * HS), BF16)] * count,
        in_specs=[in_smem()] + [anywhere()] * count,
        out_specs=[anywhere()] * count,
        scratch_shapes=[
            pltpu.VMEM((padded, 4 * HS), BF16),
            pltpu.VMEM((padded, 4 * HS), BF16),
            pltpu.VMEM((span, 128), BF16),
            pltpu.VMEM((span, 128), BF16),
            pltpu.VMEM((span, 128), BF16),
            pltpu.VMEM((span, 128), BF16),
            pltpu.VMEM((TILE, span), BF16),
            pltpu.VMEM((HS, span), F32),
            pltpu.VMEM((HS, span), F32),
            pltpu.SemaphoreType.DMA((count,)),
            pltpu.SemaphoreType.DMA((count,)),
        ],
        compiler_params=compiler_params(),
        cost_estimate=cost(3 * 10**10, 10**7, 10**7),
    )(table, *blocks)


def local_work(heads, table, local, ids_row, ids_column):
    return pl.pallas_call(
        functools.partial(local_kernel, heads),
        out_shape=jax.ShapeDtypeStruct(local.shape, BF16),
        in_specs=[in_smem(), in_vmem(), in_vmem(), in_vmem()],
        out_specs=in_vmem(),
        compiler_params=compiler_params(),
        cost_estimate=cost(5 * 10**9, 4 * 10**6, 25 * 10**5),
    )(table, local, ids_row, ids_column)


def unpack(heads, reach, table, spot, proj, gains, local, normed, cot, backs):
    rows = proj.shape[1]
    count = 2 * reach + 1
    width = heads * HS
    return pl.pallas_call(
        functools.partial(unpack_kernel, heads, reach),
        out_shape=[
            jax.ShapeDtypeStruct((rows, width), BF16),
            jax.ShapeDtypeStruct((3, rows, width), BF16),
            jax.ShapeDtypeStruct((2, 128), F32),
        ]
        + [jax.ShapeDtypeStruct((normed.shape[1], width), BF16)] * 4,
        in_specs=[in_smem()] * 2 + [in_vmem()] * 5 + [anywhere()] * count,
        out_specs=[in_vmem()] * 3 + [anywhere()] * 4,
        scratch_shapes=[
            pltpu.VMEM((4, normed.shape[1], width), BF16),
            pltpu.VMEM((count, rows, 4 * HS), BF16),
            pltpu.SemaphoreType.DMA((count,)),
        ],
        compiler_params=compiler_params(),
        cost_estimate=cost(10**9, 10**7),
    )(table, spot, proj, gains, local, normed, cot, *backs)


def on_device(
    tokens,
    image_starts,
    ln_gain,
    w_qkv,
    q_gain,
    k_gain,
    w_up,
    up_bias,
    w_attn_out,
    w_down,
    out_bias,
    cotangent,
):
    tok_rows, half = tokens.shape
    local_width = w_qkv.shape[2]
    heads = local_width // HS
    reach = (LONG_LEN + tok_rows - 2) // tok_rows
    n_seq = lax.axis_size("seq")
    place = lax.axis_index("seq")
    side = lax.axis_index("head")
    assert heads == reach + 1 and n_seq >= heads and heads % 2 == 0
    assert n_seq & (n_seq - 1) == 0 and half == local_width

    def from_peer(block):
        return lax.ppermute(block, "head", [(0, 1), (1, 0)])

    def both_halves(block):
        other = from_peer(block)
        first = jnp.where(side == 0, block, other)
        second = jnp.where(side == 0, other, block)
        return jnp.concatenate([first, second], axis=1)

    def add_over_heads(partial):
        low, high = partial[:, :half], partial[:, half:]
        send = jnp.where(side == 0, high, low).astype(BF16)
        keep = jnp.where(side == 0, low, high)
        return keep + from_peer(send).astype(F32)

    def shifted(block, distance):
        if distance == 0:
            return block
        route = [(i, i + distance) for i in range(n_seq) if 0 <= i + distance < n_seq]
        return lax.ppermute(block, "seq", route)

    gains = jnp.tile(jnp.stack([q_gain, k_gain]), (1, 2))

    gathered = both_halves(tokens)
    cot_whole = both_halves(cotangent)
    normed_f, norm_pull = jax.vjp(layer_norm, gathered.astype(F32), ln_gain)
    normed = normed_f.astype(BF16)
    proj = jnp.einsum("td,dkc->ktc", normed, w_qkv, preferred_element_type=F32)
    d_attended = jnp.einsum("td,cd->tc", cot_whole, w_attn_out, preferred_element_type=F32)
    spot = jnp.reshape(place, (1,)).astype(jnp.int32)
    packed = pack(heads, spot, proj, d_attended.astype(BF16), gains)
    packed, image_starts = lax.optimization_barrier((packed, image_starts))
    local, slots = packed[0], packed[1:]

    arrived = [shifted(slots[d % heads], d) for d in range(reach, -reach - 1, -1)]
    table = work_table(image_starts, place, n_seq, tok_rows, reach)
    row_index = jnp.arange(tok_rows, dtype=jnp.int32)
    positions = place * tok_rows + row_index
    ids = jnp.sum((image_starts[None, :] <= positions[:, None]).astype(jnp.int32), axis=1)
    is_local = (row_index >= table[0]) & (row_index < table[1])
    ids_column = jnp.where(is_local, ids, -1)[:, None]
    ids_row = jnp.where(is_local, ids, -2)[None, :]

    arrived[0], normed_ff, cot_ff = lax.optimization_barrier((arrived[0], normed, cot_whole))
    up_input = jnp.dot(normed_ff, w_up, preferred_element_type=F32) + up_bias
    hidden_f, gelu_pull = jax.vjp(exact_gelu, up_input)
    hidden = hidden_f.astype(BF16)
    d_hidden = jnp.einsum("td,fd->tf", cot_ff, w_down, preferred_element_type=F32)
    d_upper_f = gelu_pull(d_hidden)[0]
    d_upper = d_upper_f.astype(BF16)
    grad_down = jnp.einsum("tf,td->fd", hidden, cot_ff, preferred_element_type=F32)
    grad_up = jnp.einsum("td,tf->df", normed_ff, d_upper, preferred_element_type=F32)
    grad_out_bias = jnp.sum(cotangent.astype(F32), axis=0)
    grad_up_bias = jnp.sum(d_upper.astype(F32), axis=0)
    early = (grad_down.astype(BF16), grad_up.astype(BF16))
    early, arrived = lax.optimization_barrier((early, arrived))
    early = lax.psum(early, "seq")
    ffn_out = jnp.dot(hidden, w_down, preferred_element_type=F32)
    ffn_back = jnp.einsum("tf,df->td", d_upper, w_up, preferred_element_type=F32)

    worked = list(work(reach, tok_rows, table, arrived))
    worked[0], local = lax.optimization_barrier((worked[0], local))
    local_out = local_work(heads, table, local, ids_row, ids_column)
    returned = [shifted(worked[b], b - reach) for b in range(2 * reach + 1)][::-1]
    corner = jnp.bitwise_and(spot, 3)
    attended, d_proj, gain_sums, *late = unpack(
        heads, reach, table, corner, proj, gains, local_out, normed, cot_whole, returned
    )

    partial_out = jnp.dot(attended, w_attn_out, preferred_element_type=F32) + ffn_out
    summed = add_over_heads(partial_out)
    block_out = (summed + tokens.astype(F32) + out_bias).astype(BF16)
    d_normed = ffn_back + jnp.einsum("ktc,dkc->td", d_proj, w_qkv, preferred_element_type=F32)
    d_input, d_ln = norm_pull(d_normed)
    input_sum = add_over_heads(d_input)
    tokens_grad = (input_sum + cotangent.astype(F32)).astype(BF16)

    half_gain = HS // 2
    gain_total = gain_sums[:, :HS] + gain_sums[:, HS:]
    by_side = [
        jnp.concatenate([d_ln[i * half : (i + 1) * half], gain_total[:, i * half_gain : (i + 1) * half_gain].reshape(-1)])
        for i in range(2)
    ]
    own = jnp.where(side == 0, by_side[0], by_side[1])
    norms = own + from_peer(jnp.where(side == 0, by_side[1], by_side[0]))
    small = jnp.concatenate([norms, grad_up_bias, grad_out_bias])
    small_size = small.shape[0]
    small_rows = -(-small_size // (16 * half)) * 16
    small = jnp.pad(small, (0, small_rows * half - small_size)).reshape(small_rows, half)
    late = SeqSum(late, place, n_seq, small)
    for phase in range(late.phases):
        coming = late.send(phase)
        if phase == 0:
            coming, early = lax.optimization_barrier((coming, early))
        late.receive(phase, coming)
    small = late.small
    sums = late.current.astype(F32)
    width = 2 * half
    qkv_rows = 3 * width
    qkv_sum = sums[:qkv_rows].reshape(3, width, local_width).transpose(1, 0, 2)
    out_sum = jnp.concatenate(jnp.split(sums[qkv_rows:], 2, 0), axis=1)
    small = small.reshape(-1)
    at_up = half + HS
    at_out = at_up + up_bias.shape[0]
    return (
        block_out,
        tokens_grad,
        small[:half],
        qkv_sum,
        small[half : half + half_gain],
        small[half + half_gain : at_up],
        early[1].astype(F32),
        small[at_up:at_out],
        out_sum,
        early[0].astype(F32),
        small[at_out : at_out + half],
    )


def solution(mesh):
    in_specs = (
        P("seq", "head"),
        P(),
        P(),
        P(None, None, "head"),
        P(),
        P(),
        P(None, "head"),
        P("head"),
        P("head", None),
        P("head", None),
        P("head"),
        P("seq", "head"),
    )
    out_specs = (
        P("seq", "head"),
        P("seq", "head"),
        P("head"),
        P(None, None, "head"),
        P("head"),
        P("head"),
        P(None, "head"),
        P("head"),
        P("head", None),
        P("head", None),
        P("head"),
    )
    return jax.shard_map(
        on_device, mesh=mesh, in_specs=in_specs, out_specs=out_specs, check_vma=False
    )
```

```python
import functools

import jax
import jax.numpy as jnp
from jax import lax
from jax.experimental import pallas as pl
from jax.experimental.pallas import tpu as pltpu
from jax.sharding import PartitionSpec as P

HS = 64
LONG_LEN = 3136
EPSILON = 1e-06
F32 = jnp.float32
BF16 = jnp.bfloat16
TILE = 256
GROUP = 4
VMEM_LIMIT = 60 * 1024 * 1024


def layer_norm(values, gain_row):
    row_mean = jnp.mean(values, axis=-1, keepdims=True)
    centred = values - row_mean
    spread = jnp.mean(centred * centred, axis=-1, keepdims=True)
    return centred * lax.rsqrt(spread + EPSILON) * gain_row


def exact_gelu(values):
    return jax.nn.gelu(values, approximate=False)


def dot_nn(a, b):
    return lax.dot_general(a, b, (((1,), (0,)), ((), ())), preferred_element_type=F32)


def dot_nt(a, b):
    return lax.dot_general(a, b, (((1,), (1,)), ((), ())), preferred_element_type=F32)


def dot_tn(a, b):
    return lax.dot_general(a, b, (((0,), (0,)), ((), ())), preferred_element_type=F32)


def half_means(block):
    left = (lax.broadcasted_iota(jnp.int32, (256, 128), 0) % 128) // HS
    right = lax.broadcasted_iota(jnp.int32, (256, 128), 1) // HS
    averager = jnp.where(left == right, 1.0 / HS, 0.0).astype(BF16)
    coarse = block.astype(BF16)
    fine = (block - coarse.astype(F32)).astype(BF16)
    return dot_nn(jnp.concatenate([coarse, fine], axis=1), averager)


def normalized_halves(block):
    centred = block - half_means(block)
    inverse = lax.rsqrt(half_means(centred * centred) + EPSILON)
    return centred * inverse, inverse


def work_table(image_starts, place, n_seq, tok_rows, reach):
    window = reach + 1
    total = n_seq * tok_rows
    candidates = jnp.arange(2 * reach, dtype=jnp.int32) + place - reach
    positions = jnp.concatenate(
        [(candidates + 1) * tok_rows - 1, jnp.stack([place * tok_rows, (place + 1) * tok_rows - 1])]
    )
    below = image_starts[None, :] <= positions[:, None]
    starts = jnp.max(jnp.where(below, image_starts[None, :], -1), axis=1)
    ends = jnp.min(jnp.where(below, total, image_starts[None, :]), axis=1)
    first = starts // tok_rows
    last = (ends - 1) // tok_rows
    base = jnp.minimum(first, n_seq - window)
    spans = last > first
    mine = (
        (candidates >= 0)
        & (candidates < n_seq)
        & (first[:-2] == candidates)
        & spans[:-2]
        & (base[:-2] <= place)
        & (base[:-2] >= place - reach)
    )
    lengths = jnp.where(mine, ends[:-2] - starts[:-2], 0)
    rows = jnp.where(mine, starts[:-2] - (place - reach) * tok_rows, 0)
    low_end = jnp.where(spans[-2], jnp.clip(ends[-2] - place * tok_rows, 0, tok_rows), 0)
    low_end = jnp.where(first[-2] < place, low_end, 0)
    high_start = jnp.clip(starts[-1] - place * tok_rows, 0, tok_rows)
    high_start = jnp.where(last[-1] > place, high_start, tok_rows)
    head_part = jnp.stack([low_end, high_start, place - base[-2], place - base[-1]])
    turns = jnp.remainder(-base[-2:], window)
    return jnp.concatenate([head_part, rows, lengths, turns]).astype(jnp.int32)


def pack_kernel(heads, spot, proj, datt, gains, local, *refs):
    slots, sems = refs[:heads], refs[heads]
    rows = proj.shape[1]
    low = lax.broadcasted_iota(jnp.int32, (rows, 128), 1) < HS
    q_gain = gains[0:1, :] * (HS**-0.5)
    k_gain = gains[1:2, :]
    for pair in range(heads // 2):
        lanes = slice(pair * 128, (pair + 1) * 128)
        q = normalized_halves(proj[0, :, lanes])[0] * q_gain
        k = normalized_halves(proj[1, :, lanes])[0] * k_gain
        v = proj[2, :, lanes]
        d = datt[:, lanes].astype(F32)
        q, k, v = (t.astype(BF16).astype(F32) for t in (q, k, v))
        local[2 * pair, :, 0:128] = jnp.where(low, q, pltpu.roll(k, HS, 1)).astype(BF16)
        local[2 * pair, :, 128:256] = jnp.where(low, v, pltpu.roll(d, HS, 1)).astype(BF16)
        local[2 * pair + 1, :, 0:128] = jnp.where(low, pltpu.roll(q, HS, 1), k).astype(BF16)
        local[2 * pair + 1, :, 128:256] = jnp.where(low, pltpu.roll(v, HS, 1), d).astype(BF16)

    def copy_out(turn):
        return pltpu.make_async_copy(
            local.at[lax.rem(spot[0] + turn, heads)], slots[turn], sems.at[turn]
        )

    for turn in range(heads):
        copy_out(turn).start()
    for turn in range(heads):
        copy_out(turn).wait()


def softmax_tail(mixed, d_out):
    lane = lax.broadcasted_iota(jnp.int32, mixed.shape, 1)
    total = mixed[:, HS : HS + 1]
    inverse = 1.0 / jnp.where(total > 0, total, 1.0)
    mixture = mixed * inverse
    delta = jnp.sum(d_out * mixture, axis=1, keepdims=True)
    shift = -delta * inverse
    coarse = shift.astype(BF16).astype(F32)
    scaled = jnp.where(lane == HS, coarse, jnp.where(lane == HS + 1, shift - coarse, d_out * inverse))
    return mixture, scaled.astype(BF16)


def work_kernel(reach, tok_rows, max_tiles, table, *refs):
    count = 2 * reach + 1
    inputs, outputs = refs[:count], refs[count : 2 * count]
    x, y, qb, kb, vb, db, eb, dk, dv, in_sem, out_sem = refs[2 * count :]

    def copy_in(b):
        return pltpu.make_async_copy(inputs[b], x.at[pl.ds(b * tok_rows, tok_rows)], in_sem.at[b])

    def copy_out(b):
        return pltpu.make_async_copy(y.at[pl.ds(b * tok_rows, tok_rows)], outputs[b], out_sem.at[b])

    for b in range(count):
        copy_in(b).start()
    for b in range(count):
        copy_in(b).wait()
    row = lax.broadcasted_iota(jnp.int32, (TILE, 128), 0)
    lane = lax.broadcasted_iota(jnp.int32, (TILE, 128), 1)
    low = lane < HS

    @pl.loop(0, 2 * reach)
    def _(job):
        length = table[4 + 2 * reach + job]
        first = table[4 + job]
        aligned = pl.multiple_of((first // 16) * 16, 16)
        lead = first - aligned
        tiles = (lead + length + TILE - 1) // TILE
        tiles = jnp.where(length > 0, tiles, 0)
        groups = (tiles + GROUP - 1) // GROUP
        grouped = (tiles > 0) & (tiles < max_tiles)
        prepared = jnp.where(grouped, groups * GROUP, tiles)

        def inside(t):
            at = row + t * TILE
            return (at >= lead) & (at < lead + length)

        @pl.loop(0, prepared)
        def _(t):
            at = pl.multiple_of(t * TILE, TILE)
            source = pl.ds(aligned + at, TILE)
            ours = inside(t)
            keep = low & ours
            qk = x[source, 0:128].astype(F32)
            vd = x[source, 128:256].astype(F32)
            ones = jnp.where(lane < HS + 2, 1.0, 0.0)
            qb[pl.ds(at, TILE), :] = jnp.where(keep, qk, 0.0).astype(BF16)
            kb[pl.ds(at, TILE), :] = jnp.where(keep, pltpu.roll(qk, HS, 1), 0.0).astype(BF16)
            vb[pl.ds(at, TILE), :] = jnp.where(ours, jnp.where(low, vd, ones), 0.0).astype(BF16)
            db[pl.ds(at, TILE), :] = jnp.where(keep, pltpu.roll(vd, HS, 1), 0.0).astype(BF16)
            dk[:, pl.ds(at, TILE)] = jnp.zeros((HS, TILE), F32)
            dv[:, pl.ds(at, TILE)] = jnp.zeros((HS, TILE), F32)

        def store(t, lanes, value):
            place = pl.ds(aligned + pl.multiple_of(t * TILE, TILE), TILE)
            old = y[place, lanes].astype(F32)
            y[place, lanes] = jnp.where(inside(t), value, old).astype(BF16)

        def first_pass(q, at):
            e = jnp.exp(dot_nt(q, kb[at, :])).astype(BF16)
            eb[:, at] = e

        def second_pass(q, scaled, at):
            e = eb[:, at]
            dv[:, at] += dot_tn(scaled[:, :HS], e)
            grad = dot_nt(scaled, vb[at, :])
            ds = (e.astype(F32) * grad).astype(BF16)
            eb[:, at] = ds
            dk[:, at] += dot_tn(q[:, :HS], ds)

        @pl.when(tiles == max_tiles)
        def _():
            @pl.loop(0, max_tiles)
            def _(t):
                at = pl.ds(pl.multiple_of(t * TILE, TILE), TILE)
                q = qb[at, :]
                for s in range(max_tiles):
                    first_pass(q, slice(s * TILE, (s + 1) * TILE))
                mixture, scaled = softmax_tail(dot_nn(eb[...], vb[...]), db[at, :].astype(F32))
                for s in range(max_tiles):
                    second_pass(q, scaled, slice(s * TILE, (s + 1) * TILE))
                d_query = dot_nn(eb[...], kb[...])
                store(t, slice(0, 128), jnp.where(low, mixture, pltpu.roll(d_query, HS, 1)))

        @pl.when(grouped)
        def _():
            @pl.loop(0, tiles)
            def _(t):
                at = pl.ds(pl.multiple_of(t * TILE, TILE), TILE)
                q = qb[at, :]

                def mix(g, total):
                    for s in range(GROUP):
                        first_pass(q, pl.ds(pl.multiple_of((g * GROUP + s) * TILE, TILE), TILE))
                    to = pl.ds(pl.multiple_of(g * GROUP * TILE, GROUP * TILE), GROUP * TILE)
                    return total + dot_nn(eb[:, to], vb[to, :])

                mixed = lax.fori_loop(0, groups, mix, jnp.zeros((TILE, 128), F32))
                mixture, scaled = softmax_tail(mixed, db[at, :].astype(F32))

                def back(g, total):
                    for s in range(GROUP):
                        to = pl.ds(pl.multiple_of((g * GROUP + s) * TILE, TILE), TILE)
                        second_pass(q, scaled, to)
                    to = pl.ds(pl.multiple_of(g * GROUP * TILE, GROUP * TILE), GROUP * TILE)
                    return total + dot_nn(eb[:, to], kb[to, :])

                d_query = lax.fori_loop(0, groups, back, jnp.zeros((TILE, 128), F32))
                store(t, slice(0, 128), jnp.where(low, mixture, pltpu.roll(d_query, HS, 1)))

        @pl.loop(0, tiles)
        def _(t):
            at = pl.ds(pl.multiple_of(t * TILE, TILE), TILE)
            both = jnp.concatenate([dk[:, at], dv[:, at]], axis=0)
            store(t, slice(128, 256), both.T)

    for b in range(count):
        copy_out(b).start()
    for b in range(count):
        copy_out(b).wait()


def local_kernel(heads, table, local, ids_row, ids_column, out):
    rows = local.shape[1]

    @pl.when(table[0] < table[1])
    def _():
        lane = lax.broadcasted_iota(jnp.int32, (rows, 128), 1)
        low = lane < HS
        same = (ids_column[...] == ids_row[...]).astype(F32)
        ones = jnp.where(lane < HS + 2, 1.0, 0.0)

        @pl.loop(0, heads)
        def _(h):
            qk = local[h, :, 0:128].astype(F32)
            vd = local[h, :, 128:256].astype(F32)
            q = jnp.where(low, qk, 0.0).astype(BF16)
            k = jnp.where(low, pltpu.roll(qk, HS, 1), 0.0).astype(BF16)
            v = jnp.where(low, vd, ones).astype(BF16)
            d_out = jnp.where(low, pltpu.roll(vd, HS, 1), 0.0)
            e = (jnp.exp(dot_nt(q, k)) * same).astype(BF16)
            mixture, scaled = softmax_tail(dot_nn(e, v), d_out)
            ds = (e.astype(F32) * dot_nt(scaled, v)).astype(BF16)
            d_query = dot_nn(ds, k)
            d_key = dot_tn(q[:, :HS], ds)
            d_value = dot_tn(scaled[:, :HS], e)
            out[h, :, 0:128] = jnp.where(low, mixture, pltpu.roll(d_query, HS, 1)).astype(BF16)
            out[h, :, 128:256] = jnp.concatenate([d_key, d_value], axis=0).T.astype(BF16)


def unpack_kernel(heads, reach, table, spot, proj, gains, local, normed, cot, *refs):
    count = 2 * reach + 1
    backs = refs[:count]
    attended, d_proj, gain_sums = refs[count : count + 3]
    blocks = refs[count + 3 : count + 7]
    grads, stacked, sems = refs[count + 7 :]
    rows = proj.shape[1]

    def copy_in(b):
        return pltpu.make_async_copy(backs[b], stacked.at[b], sems.at[b])

    for b in range(count):
        copy_in(b).start()
    for b in range(count):
        copy_in(b).wait()
    low = lax.broadcasted_iota(jnp.int32, (rows, 128), 1) < HS
    row = lax.broadcasted_iota(jnp.int32, (rows, 256), 0)
    from_low = row < table[0]
    from_high = row >= table[1]
    q_gain = gains[0:1, :] * (HS**-0.5)
    k_gain = gains[1:2, :]

    def gathered(h):
        lower = stacked[lax.rem(h + table[4 + 4 * reach], heads) - table[2] + reach].astype(F32)
        upper = stacked[lax.rem(h + table[5 + 4 * reach], heads) - table[3] + reach].astype(F32)
        return jnp.where(from_low, lower, jnp.where(from_high, upper, local[h].astype(F32)))

    def back(raw, gradient, gain):
        hat, inverse = normalized_halves(raw)
        scaled = gradient * gain
        shifted = scaled - half_means(scaled) - hat * half_means(scaled * hat)
        return shifted * inverse, jnp.sum(gradient * hat, axis=0, keepdims=True)

    q_sum = jnp.zeros((1, 128), F32)
    k_sum = jnp.zeros((1, 128), F32)
    for pair in range(heads // 2):
        lanes = slice(pair * 128, (pair + 1) * 128)
        even, odd = gathered(2 * pair), gathered(2 * pair + 1)
        mixture = jnp.where(low, even[:, 0:128], pltpu.roll(odd[:, 0:128], HS, 1))
        d_query = jnp.where(low, pltpu.roll(even[:, 0:128], HS, 1), odd[:, 0:128])
        d_key = jnp.where(low, even[:, 128:256], pltpu.roll(odd[:, 128:256], HS, 1))
        d_value = jnp.where(low, pltpu.roll(even[:, 128:256], HS, 1), odd[:, 128:256])
        attended[:, lanes] = mixture.astype(BF16)
        q_raw, q_part = back(proj[0, :, lanes], d_query, q_gain)
        k_raw, k_part = back(proj[1, :, lanes], d_key, k_gain)
        q_sum += q_part
        k_sum += k_part
        d_proj[0, :, lanes] = q_raw.astype(BF16)
        d_proj[1, :, lanes] = k_raw.astype(BF16)
        d_proj[2, :, lanes] = d_value.astype(BF16)
    gain_sums[...] = jnp.concatenate([q_sum * (HS**-0.5), k_sum], axis=0)
    width, columns = normed.shape[1], heads * HS

    for part in range(4):
        if part < 3:
            grads[part] = dot_tn(normed[...], d_proj[part]).astype(BF16)
        else:
            for at in range(0, width, columns):
                grads[part, at : at + columns, :] = dot_tn(
                    attended[...], cot[:, at : at + columns]
                ).astype(BF16)
    for index, block in enumerate(blocks):
        pltpu.make_async_copy(grads.at[index ^ spot[0]], block, sems.at[index]).start()
    for index, block in enumerate(blocks):
        pltpu.make_async_copy(grads.at[index ^ spot[0]], block, sems.at[index]).wait()


class SeqSum:
    def __init__(self, blocks, place, n_seq, small=None):
        width = n_seq.bit_length() - 1
        self.n_seq = n_seq
        stages = [(bit, 1 << min(2, width - bit)) for bit in range(0, width, 2)]
        self.order = stages + stages[::-1]
        self.phases = len(self.order)
        self.codes = {bit: (place >> bit) & (radix - 1) for bit, radix in stages}
        self.blocks, self.current, self.small = blocks, None, small

    def describe(self, phase):
        bit, radix = self.order[phase]
        adding = phase < self.phases // 2
        joins = self.small is not None and adding == (bit > 0)
        return bit, radix, adding, joins, self.codes[bit]

    def block(self, phase, mask):
        bit, radix, _, _, code = self.describe(phase)
        if phase == 0:
            return self.blocks[mask]
        rows, lanes = self.current.shape
        split = self.current.reshape(radix, rows // radix, lanes)
        return lax.dynamic_index_in_dim(split, code ^ mask, 0, keepdims=False)

    def send(self, phase):
        bit, radix, adding, joins, code = self.describe(phase)
        tail = self.small.astype(BF16) if joins else None
        arrived = []
        for mask in reversed(range(1, radix)):
            block = self.current
            if adding:
                block = self.block(phase, mask)
            if joins:
                block = jnp.concatenate([block, tail], axis=0)
            route = [(i, i ^ (mask << bit)) for i in range(self.n_seq)]
            arrived.append(lax.ppermute(block, "seq", route))
        return arrived

    def receive(self, phase, arrived):
        bit, radix, adding, joins, code = self.describe(phase)
        own = self.block(phase, 0) if adding else self.current
        height, lanes = own.shape
        if adding:
            total = own.astype(F32)
            for block in arrived:
                total = total + block[:height].astype(F32)
            self.current = total.astype(BF16)
        else:
            whole = jnp.zeros((radix, height, lanes), BF16)
            whole = lax.dynamic_update_index_in_dim(whole, self.current, code, 0)
            for mask, block in zip(reversed(range(1, radix)), arrived):
                whole = lax.dynamic_update_index_in_dim(whole, block[:height], code ^ mask, 0)
            self.current = whole.reshape(radix * height, lanes)
        if joins:
            small = self.small.astype(BF16).astype(F32)
            for block in arrived:
                small = small + block[height:].astype(F32)
            self.small = small


def in_vmem():
    return pl.BlockSpec(memory_space=pltpu.VMEM)


def in_smem():
    return pl.BlockSpec(memory_space=pltpu.SMEM)


def anywhere():
    return pl.BlockSpec(memory_space=pl.ANY)


def compiler_params():
    return pltpu.CompilerParams(vmem_limit_bytes=VMEM_LIMIT)


def cost(flops, bytes_accessed, transcendentals=0):
    return pl.CostEstimate(
        flops=flops, bytes_accessed=bytes_accessed, transcendentals=transcendentals
    )


def pack(heads, spot, proj, datt, gains):
    rows = proj.shape[1]
    slot = jax.ShapeDtypeStruct((rows, 4 * HS), BF16)
    return pl.pallas_call(
        functools.partial(pack_kernel, heads),
        out_shape=[jax.ShapeDtypeStruct((heads, rows, 4 * HS), BF16)] + [slot] * heads,
        in_specs=[in_smem(), in_vmem(), in_vmem(), in_vmem()],
        out_specs=[in_vmem()] + [anywhere()] * heads,
        scratch_shapes=[pltpu.SemaphoreType.DMA((heads,))],
        compiler_params=compiler_params(),
        cost_estimate=cost(10**9, 10**7),
    )(spot, proj, datt, gains)


def work(reach, tok_rows, table, blocks):
    count = 2 * reach + 1
    max_tiles = -(-(LONG_LEN + 15) // TILE)
    padded = count * tok_rows + GROUP * TILE
    span = max_tiles * TILE
    return pl.pallas_call(
        functools.partial(work_kernel, reach, tok_rows, max_tiles),
        out_shape=[jax.ShapeDtypeStruct((tok_rows, 4 * HS), BF16)] * count,
        in_specs=[in_smem()] + [anywhere()] * count,
        out_specs=[anywhere()] * count,
        scratch_shapes=[
            pltpu.VMEM((padded, 4 * HS), BF16),
            pltpu.VMEM((padded, 4 * HS), BF16),
            pltpu.VMEM((span, 128), BF16),
            pltpu.VMEM((span, 128), BF16),
            pltpu.VMEM((span, 128), BF16),
            pltpu.VMEM((span, 128), BF16),
            pltpu.VMEM((TILE, span), BF16),
            pltpu.VMEM((HS, span), F32),
            pltpu.VMEM((HS, span), F32),
            pltpu.SemaphoreType.DMA((count,)),
            pltpu.SemaphoreType.DMA((count,)),
        ],
        compiler_params=compiler_params(),
        cost_estimate=cost(3 * 10**10, 10**7, 10**7),
    )(table, *blocks)


def local_work(heads, table, local, ids_row, ids_column):
    return pl.pallas_call(
        functools.partial(local_kernel, heads),
        out_shape=jax.ShapeDtypeStruct(local.shape, BF16),
        in_specs=[in_smem(), in_vmem(), in_vmem(), in_vmem()],
        out_specs=in_vmem(),
        compiler_params=compiler_params(),
        cost_estimate=cost(5 * 10**9, 4 * 10**6, 25 * 10**5),
    )(table, local, ids_row, ids_column)


def unpack(heads, reach, table, spot, proj, gains, local, normed, cot, backs):
    rows = proj.shape[1]
    count = 2 * reach + 1
    width = heads * HS
    return pl.pallas_call(
        functools.partial(unpack_kernel, heads, reach),
        out_shape=[
            jax.ShapeDtypeStruct((rows, width), BF16),
            jax.ShapeDtypeStruct((3, rows, width), BF16),
            jax.ShapeDtypeStruct((2, 128), F32),
        ]
        + [jax.ShapeDtypeStruct((normed.shape[1], width), BF16)] * 4,
        in_specs=[in_smem()] * 2 + [in_vmem()] * 5 + [anywhere()] * count,
        out_specs=[in_vmem()] * 3 + [anywhere()] * 4,
        scratch_shapes=[
            pltpu.VMEM((4, normed.shape[1], width), BF16),
            pltpu.VMEM((count, rows, 4 * HS), BF16),
            pltpu.SemaphoreType.DMA((count,)),
        ],
        compiler_params=compiler_params(),
        cost_estimate=cost(10**9, 10**7),
    )(table, spot, proj, gains, local, normed, cot, *backs)


def on_device(
    tokens,
    image_starts,
    ln_gain,
    w_qkv,
    q_gain,
    k_gain,
    w_up,
    up_bias,
    w_attn_out,
    w_down,
    out_bias,
    cotangent,
):
    tok_rows, half = tokens.shape
    local_width = w_qkv.shape[2]
    heads = local_width // HS
    reach = (LONG_LEN + tok_rows - 2) // tok_rows
    n_seq = lax.axis_size("seq")
    place = lax.axis_index("seq")
    side = lax.axis_index("head")
    assert heads == reach + 1 and n_seq >= heads and heads % 2 == 0
    assert n_seq & (n_seq - 1) == 0 and half == local_width

    def from_peer(block):
        return lax.ppermute(block, "head", [(0, 1), (1, 0)])

    def both_halves(block):
        other = from_peer(block)
        first = jnp.where(side == 0, block, other)
        second = jnp.where(side == 0, other, block)
        return jnp.concatenate([first, second], axis=1)

    def add_over_heads(partial):
        low, high = partial[:, :half], partial[:, half:]
        send = jnp.where(side == 0, high, low).astype(BF16)
        keep = jnp.where(side == 0, low, high)
        return keep + from_peer(send).astype(F32)

    def shifted(block, distance):
        if distance == 0:
            return block
        route = [(i, i + distance) for i in range(n_seq) if 0 <= i + distance < n_seq]
        return lax.ppermute(block, "seq", route)

    gains = jnp.tile(jnp.stack([q_gain, k_gain]), (1, 2))

    gathered = both_halves(tokens)
    cot_whole = both_halves(cotangent)
    normed_f, norm_pull = jax.vjp(layer_norm, gathered.astype(F32), ln_gain)
    normed = normed_f.astype(BF16)
    proj = jnp.einsum("td,dkc->ktc", normed, w_qkv, preferred_element_type=F32)
    d_attended = jnp.einsum("td,cd->tc", cot_whole, w_attn_out, preferred_element_type=F32)
    spot = jnp.reshape(place, (1,)).astype(jnp.int32)
    packed = pack(heads, spot, proj, d_attended.astype(BF16), gains)
    packed, image_starts = lax.optimization_barrier((packed, image_starts))
    local, slots = packed[0], packed[1:]

    arrived = [shifted(slots[d % heads], d) for d in range(reach, -reach - 1, -1)]
    table = work_table(image_starts, place, n_seq, tok_rows, reach)
    row_index = jnp.arange(tok_rows, dtype=jnp.int32)
    positions = place * tok_rows + row_index
    ids = jnp.sum((image_starts[None, :] <= positions[:, None]).astype(jnp.int32), axis=1)
    is_local = (row_index >= table[0]) & (row_index < table[1])
    ids_column = jnp.where(is_local, ids, -1)[:, None]
    ids_row = jnp.where(is_local, ids, -2)[None, :]

    arrived[0], normed_ff, cot_ff = lax.optimization_barrier((arrived[0], normed, cot_whole))
    up_input = jnp.dot(normed_ff, w_up, preferred_element_type=F32) + up_bias
    hidden_f, gelu_pull = jax.vjp(exact_gelu, up_input)
    hidden = hidden_f.astype(BF16)
    d_hidden = jnp.einsum("td,fd->tf", cot_ff, w_down, preferred_element_type=F32)
    d_upper_f = gelu_pull(d_hidden)[0]
    d_upper = d_upper_f.astype(BF16)
    grad_down = jnp.einsum("tf,td->fd", hidden, cot_ff, preferred_element_type=F32)
    grad_up = jnp.einsum("td,tf->df", normed_ff, d_upper, preferred_element_type=F32)
    grad_out_bias = jnp.sum(cotangent.astype(F32), axis=0)
    grad_up_bias = jnp.sum(d_upper.astype(F32), axis=0)
    early = (grad_down.astype(BF16), grad_up.astype(BF16))
    early, arrived = lax.optimization_barrier((early, arrived))
    early = lax.psum(early, "seq")
    ffn_out = jnp.dot(hidden, w_down, preferred_element_type=F32)
    ffn_back = jnp.einsum("tf,df->td", d_upper, w_up, preferred_element_type=F32)

    worked = list(work(reach, tok_rows, table, arrived))
    worked[0], local = lax.optimization_barrier((worked[0], local))
    local_out = local_work(heads, table, local, ids_row, ids_column)
    returned = [shifted(worked[b], b - reach) for b in range(2 * reach + 1)][::-1]
    corner = jnp.bitwise_and(spot, 3)
    attended, d_proj, gain_sums, *late = unpack(
        heads, reach, table, corner, proj, gains, local_out, normed, cot_whole, returned
    )

    partial_out = jnp.dot(attended, w_attn_out, preferred_element_type=F32) + ffn_out
    summed = add_over_heads(partial_out)
    block_out = (summed + tokens.astype(F32) + out_bias).astype(BF16)
    d_normed = ffn_back + jnp.einsum("ktc,dkc->td", d_proj, w_qkv, preferred_element_type=F32)
    d_input, d_ln = norm_pull(d_normed)
    input_sum = add_over_heads(d_input)
    tokens_grad = (input_sum + cotangent.astype(F32)).astype(BF16)

    half_gain = HS // 2
    gain_total = gain_sums[:, :HS] + gain_sums[:, HS:]
    by_side = [
        jnp.concatenate([d_ln[i * half : (i + 1) * half], gain_total[:, i * half_gain : (i + 1) * half_gain].reshape(-1)])
        for i in range(2)
    ]
    own = jnp.where(side == 0, by_side[0], by_side[1])
    norms = own + from_peer(jnp.where(side == 0, by_side[1], by_side[0]))
    small = jnp.concatenate([norms, grad_up_bias, grad_out_bias])
    small_size = small.shape[0]
    small_rows = -(-small_size // (16 * half)) * 16
    small = jnp.pad(small, (0, small_rows * half - small_size)).reshape(small_rows, half)
    late = SeqSum(late, place, n_seq, small)
    for phase in range(late.phases):
        coming = late.send(phase)
        if phase == 0:
            coming, early = lax.optimization_barrier((coming, early))
        late.receive(phase, coming)
    small = late.small
    sums = late.current.astype(F32)
    width = 2 * half
    qkv_rows = 3 * width
    qkv_sum = sums[:qkv_rows].reshape(3, width, local_width).transpose(1, 0, 2)
    out_sum = jnp.concatenate(jnp.split(sums[qkv_rows:], 2, 0), axis=1)
    small = small.reshape(-1)
    at_up = half + HS
    at_out = at_up + up_bias.shape[0]
    return (
        block_out,
        tokens_grad,
        small[:half],
        qkv_sum,
        small[half : half + half_gain],
        small[half + half_gain : at_up],
        early[1].astype(F32),
        small[at_up:at_out],
        out_sum,
        early[0].astype(F32),
        small[at_out : at_out + half],
    )


def solution(mesh):
    in_specs = (
        P("seq", "head"),
        P(),
        P(),
        P(None, None, "head"),
        P(),
        P(),
        P(None, "head"),
        P("head"),
        P("head", None),
        P("head", None),
        P("head"),
        P("seq", "head"),
    )
    out_specs = (
        P("seq", "head"),
        P("seq", "head"),
        P("head"),
        P(None, None, "head"),
        P("head"),
        P("head"),
        P(None, "head"),
        P("head"),
        P("head", None),
        P("head", None),
        P("head"),
    )
    return jax.shard_map(
        on_device, mesh=mesh, in_specs=in_specs, out_specs=out_specs, check_vma=False
    )
```
